512 devices in a mesh: gx: 32 (over z, core), gy: 8 (over x_lo, y), vert: 2 (over x_hi).
Axes of the slice: x: 4 (x_hi: 2, x_lo: 2; x = x_hi * 2 + x_lo), y: 4, z: 16, core: 2. Of those that a mesh axis runs over, the one named last changes fastest.
Arguments:
- vectors: float32 [16, 256, 64, 128], P('vert', 'gx', 'gy'), may hold values from -6 to 6
- conductivity: float32 [256, 64, 128], P('gx', 'gy'), may hold values from 0.3 to 3
- c_points: int32 [256, 64, 16], P('gx', 'gy'), may hold values from -1 to 127, as said below
Outputs:
- interp: float32 [256, 64, 16, 128], P('gx', 'gy')
- coarse: float32 [256, 64, 9, 256], P('gx', 'gy')
The draws below stay inside these ranges and needn't reach their ends.
Inputs may be any that keep to these rules, and one draw needn't show every extreme that they name: `c_points`: in each tile column the used slots come first, hold distinct positions in increasing order, and number at least 8; some column uses all 16 slots.
All inputs are finite; a program needn't handle non-finite values.
Results may differ from the reference program's by a relative error of at most 0.0003.
Values sent between devices are 32-bit elements; how exact they have to be, the bound alone decides.
No kernel may reach another device: no remote copies, remote signals or barrier semaphores. Data moves between devices by JAX's collectives and lax.ppermute only.
A program may use at most 64 MiB of HBM per device.

```python
import math
import jax
import jax.numpy as jnp
from jax import lax

NZ = 128
VECS = 16
CPTS = 16
SWEEPS = 3
NX = 256
NY = 64


def draw_c_points(key, part):
    columns = NX * NY
    keys = jax.random.split(jax.random.fold_in(key, 11), columns)
    chosen = jax.vmap(lambda single: jax.random.permutation(single, NZ)[:CPTS])(keys)
    chosen = jnp.sort(chosen.astype(jnp.int32), axis=1)
    counts = jax.random.randint(jax.random.fold_in(key, 23), (columns,), CPTS // 2, CPTS + 1)
    counts = counts.at[0].set(CPTS)
    slots = jnp.arange(CPTS, dtype=jnp.int32)[None, :]
    result = jnp.where(slots < counts[:, None], chosen, -1)
    return result.reshape(NX, NY, CPTS).astype(jnp.int32)


def level_of(stream_key, dims, pieces, least, largest):
    gain = 1.0
    for dim, parts in pieces:
        heights = jax.random.uniform(jax.random.fold_in(jax.random.fold_in(stream_key, 6), dim), (parts,), jnp.float32, least / len(pieces), largest / len(pieces))
        gain = gain * jnp.repeat(jnp.exp(heights), dims[dim] // parts).reshape((-1,) + (1,) * (len(dims) - 1 - dim))
    return gain


def scatter_about(rng, extent, spread, most, cuts=(), kind=jnp.bfloat16):
    loudness = level_of(rng, extent, cuts, -0.22, 0.18) if cuts else 1.0
    values = jax.random.normal(rng, extent, jnp.float32) * spread * loudness
    return jnp.minimum(jnp.maximum(values, -most), most).astype(kind)


def setup_inputs(seed: int = 0) -> dict:
    streams_of = jax.random.split(jax.random.key(seed), 4)
    return {
        "vectors": scatter_about(streams_of[0], (VECS, NX, NY, NZ), 1.0, 6.0, ((0, 2), (1, 32), (2, 8)), jnp.float32),
        "conductivity": jnp.clip(jnp.exp(math.log(3.0) - 2.3025851 * jax.random.uniform(streams_of[1], (NX, NY, NZ), jnp.float32) ** level_of(streams_of[1], (NX, NY, NZ), ((0, 32), (1, 8)), -0.2, 0.2)), 0.3, 3.0),
        "c_points": draw_c_points(jax.random.fold_in(streams_of[3], 71), 0),
    }


ANISOTROPY = (1.0, 0.6, 0.15)
OMEGA = 0.6
SHIFT = 0.5
RIDGE = 0.1

def stencil_offsets():
    result = []
    for move_x in (-1, 0, 1):
        for move_y in (-1, 0, 1):
            for move_z in (-1, 0, 1):
                if move_x != 0 or move_y != 0 or move_z != 0:
                    result.append((move_x, move_y, move_z))
    return result

def coupling(move):
    weight = 1.0
    for axis_no in range(3):
        if move[axis_no] != 0:
            weight = weight * ANISOTROPY[axis_no]
    return weight

def window_of(move, shape):
    return tuple((slice(1 + move[axis_no], 1 + move[axis_no] + shape[axis_no]) for axis_no in range(3)))

def operator_apply(padded, kpad):
    shape = (kpad.shape[0] - 2, kpad.shape[1] - 2, kpad.shape[2] - 2)
    interior = kpad[1:-1, 1:-1, 1:-1]
    centre = padded[:, 1:-1, 1:-1, 1:-1]
    diagonal = SHIFT * interior * interior
    nearby = jnp.zeros_like(centre)
    for move in stencil_offsets():
        window = window_of(move, shape)
        couple = coupling(move) * interior * kpad[window]
        diagonal = diagonal + couple
        nearby = nearby + couple * padded[(slice(None),) + window]
    return (diagonal * centre - nearby, diagonal, centre)

def jacobi(padded, kpad):
    image, diagonal, centre = operator_apply(padded, kpad)
    alive = diagonal > 0.0
    guarded = jnp.where(alive, diagonal, 1.0)
    return jnp.where(alive, centre - OMEGA * image / guarded, 0.0)

def gram_terms(field, c_points):
    depth = field.shape[-1]
    onehot = (c_points[..., None] == jnp.arange(depth, dtype=jnp.int32)).astype(jnp.float32)
    cvals = jnp.einsum('vxyz,xyjz->vxyj', field, onehot, precision=lax.Precision.HIGHEST)
    right = jnp.einsum('vxyz,vxyj->xyjz', field, cvals, precision=lax.Precision.HIGHEST)
    gram = jnp.einsum('vxyi,vxyj->xyij', cvals, cvals, precision=lax.Precision.HIGHEST)
    return (right, gram, onehot)

def solve_interp(right, gram, onehot):
    slots = gram.shape[-1]
    ridge = RIDGE * jnp.trace(gram, axis1=2, axis2=3) / slots + 1e-06
    system = gram + ridge[:, :, None, None] * jnp.eye(slots, dtype=jnp.float32)
    lower = jnp.linalg.cholesky(system)
    weights = jax.scipy.linalg.cho_solve((lower, True), right)
    c_row = jnp.sum(onehot, axis=2)
    return weights * (1.0 - c_row[:, :, None, :]) + onehot

def galerkin(interp, ppad, kpad):
    shape = (kpad.shape[0] - 2, kpad.shape[1] - 2, kpad.shape[2] - 2)
    interior = kpad[1:-1, 1:-1, 1:-1]
    diagonal = SHIFT * interior * interior
    for move in stencil_offsets():
        diagonal = diagonal + coupling(move) * interior * kpad[window_of(move, shape)]
    blocks = []
    slots = interp.shape[2]
    for move_x in (-1, 0, 1):
        for move_y in (-1, 0, 1):
            if move_x == 0 and move_y == 0:
                image = diagonal[:, :, None, :] * interp
            else:
                image = jnp.zeros_like(interp)
            for move_z in (-1, 0, 1):
                if move_x == 0 and move_y == 0 and (move_z == 0):
                    continue
                move = (move_x, move_y, move_z)
                window = window_of(move, shape)
                couple = coupling(move) * interior * kpad[window]
                source = ppad[window[0], window[1], :, window[2]]
                image = image - couple[:, :, None, :] * source
            block = jnp.einsum('xyiz,xyjz->xyij', interp, image, precision=lax.Precision.HIGHEST)
            blocks.append(block.reshape(shape[0], shape[1], slots * slots))
    return jnp.stack(blocks, axis=2)

def reference(vectors, conductivity, c_points):
    kpad = jnp.pad(conductivity, 1)
    field = vectors
    for turn in range(SWEEPS):
        field = jacobi(jnp.pad(field, ((0, 0), (1, 1), (1, 1), (1, 1))), kpad)
    right, gram, onehot = gram_terms(field, c_points)
    interp = solve_interp(right, gram, onehot)
    ppad = jnp.pad(interp, ((1, 1), (1, 1), (0, 0), (1, 1)))
    coarse = galerkin(interp, ppad, kpad)
    return (interp, coarse)
```

```python
import jax
import jax.numpy as jnp
from jax import lax
from jax.experimental import pallas as pl
from jax.experimental.pallas import tpu as pltpu
from jax.sharding import PartitionSpec as P

WY = 0.6
WZ = 0.15
OMEGA = 0.6
SHIFT = 0.5
RIDGE = 0.1
F32 = jnp.float32
BF16 = jnp.bfloat16
VMEM = pltpu.VMEM
SLAB = (37, 8, 128)


def iota(shape, dim):
    return lax.broadcasted_iota(jnp.int32, shape, dim)


def along_z(t, low, high):
    return t + low * pltpu.roll(t, 1, 1) + high * pltpu.roll(t, 127, 1)


def z_weights(rows):
    lane = iota((rows, 128), 1)
    return jnp.where(lane == 0, 0.0, WZ), jnp.where(lane == 127, 0.0, WZ)


def pack_kernel(vec, cond, points, tiles, ylow, yhigh, xlow, xhigh, padded):
    for x in range(8):
        for y in range(8):
            t = vec[pl.ds(x * 8 + y, 8, stride=64), :]
            tiles[x * 8 + y] = t
            if y < 4:
                ylow[x * 4 + y] = t
            else:
                yhigh[x * 4 + y - 4] = t
            if x < 4:
                xlow[x * 8 + y] = t
            else:
                xhigh[(x - 4) * 8 + y] = t
    padded[...] = jnp.full((64, 128), -1.0, F32)
    padded[:, 0:16] = points[...].astype(F32)
    for t in range(4):
        for half in range(2):
            x = 2 * t + half
            ylow[32 + t, half * 4 : half * 4 + 4, :] = cond[x * 8 : x * 8 + 4, :]
            yhigh[32 + t, half * 4 : half * 4 + 4, :] = cond[x * 8 + 4 : x * 8 + 8, :]
        xlow[32 + t] = cond[t * 8 : t * 8 + 8, :]
        xhigh[32 + t] = cond[t * 8 + 32 : t * 8 + 40, :]
    ylow[36] = padded[pl.ds(0, 8, stride=8), :]
    yhigh[36] = padded[pl.ds(7, 8, stride=8), :]
    xlow[36] = padded[0:8, :]
    xhigh[36] = padded[56:64, :]


def corner_kernel(ylow, yhigh, low, high):
    for out, x in ((low, 0), (high, 1)):
        out[0:16] = ylow[16 * x : 16 * x + 16]
        out[16:32] = yhigh[16 * x : 16 * x + 16]
        out[32:34] = ylow[32 + 2 * x : 34 + 2 * x]
        out[34:36] = yhigh[32 + 2 * x : 34 + 2 * x]
        out[36] = jnp.zeros((8, 128), F32)
        out[36, 0:1, :] = ylow[36, 7 * x : 7 * x + 1, :]
        out[36, 1:2, :] = yhigh[36, 7 * x : 7 * x + 1, :]


def sweep_kernel(
    tiles, cond, padded, ylow, yhigh, xlow, xhigh, clow, chigh,
    field, k_out, e_out, c_out,
    u0, u1, kk, kz, hh, h4, rk, ee,
):
    for x in range(16):
        for part, y0, n in ((0, 0, 4), (1, 4, 8), (2, 12, 4)):
            if 4 <= x < 12:
                if part == 1:
                    rows = cond[(x - 4) * 8 : (x - 4) * 8 + 8, :]
                else:
                    src = ylow if part == 0 else yhigh
                    half = (x - 4) % 2 * 4
                    rows = src[32 + (x - 4) // 2, half : half + 4, :]
            else:
                xx = x if x < 4 else x - 12
                if part == 1:
                    rows = (xlow if x < 4 else xhigh)[32 + xx]
                else:
                    src = clow if x < 4 else chigh
                    half = xx % 2 * 4
                    rows = src[32 + part + xx // 2, half : half + 4, :]
            kk[x, y0 : y0 + n, :] = rows

    low16, high16 = z_weights(16)
    for x in range(16):
        kz[x] = along_z(kk[x], low16, high16)
    for x in range(1, 15):
        k = kk[x]
        s = kz[x - 1] + kz[x] + kz[x + 1]
        s = s + WY * (pltpu.roll(s, 1, 0) + pltpu.roll(s, 15, 0)) - k
        alive = k > 0.0
        h = jnp.where(alive, OMEGA * k / jnp.where(alive, SHIFT * k + s, 1.0), 0.0)
        hh[x] = h
        h4[x] = (1.0 - OMEGA) - h
        rk[x] = jnp.where(alive, 1.0 / jnp.where(alive, k, 1.0), 0.0)
        ee[x] = (SHIFT + 1.0) * k + s

    for x in range(16):
        for y in range(16):
            inner_x, inner_y = 4 <= x < 12, 4 <= y < 12
            if inner_x and inner_y:
                t = tiles[(x - 4) * 8 + y - 4]
            elif inner_x:
                t = (ylow if y < 4 else yhigh)[(x - 4) * 4 + (y if y < 4 else y - 12)]
            else:
                xx = x if x < 4 else x - 12
                if inner_y:
                    t = (xlow if x < 4 else xhigh)[xx * 8 + y - 4]
                else:
                    src = clow if x < 4 else chigh
                    t = src[xx * 4 + (y if y < 4 else 16 + y - 12)]
            u0[x, y] = t * jnp.broadcast_to(kk[x, y : y + 1, :], (8, 128))

    low8, high8 = z_weights(8)

    def sweep(src, first, count, write):
        def step(x, carry):
            hx, h4x = hh[x], h4[x]
            s = [
                src[x - 1, y] + src[x, y] + src[x + 1, y]
                for y in range(first - 1, first + count + 1)
            ]
            for j in range(count):
                y = first + j
                t = s[j + 1] + WY * (s[j] + s[j + 2])
                w = along_z(t, low8, high8)
                a = jnp.broadcast_to(h4x[y : y + 1, :], (8, 128))
                b = jnp.broadcast_to(hx[y : y + 1, :], (8, 128))
                write(x, y, a * src[x, y] + b * w)
            return carry

        lax.fori_loop(first, first + count, step, 0)

    def to_u1(x, y, value):
        u1[x, y] = value

    def to_u0(x, y, value):
        u0[x, y] = value

    sweep(u0, 1, 14, to_u1)
    sweep(u1, 2, 12, to_u0)

    def step(x, carry):
        hx, h4x, rx = hh[x], h4[x], rk[x]
        s = [u0[x - 1, y] + u0[x, y] + u0[x + 1, y] for y in range(2, 14)]
        for j in range(10):
            y = 3 + j
            t = s[j + 1] + WY * (s[j] + s[j + 2])
            w = along_z(t, low8, high8)
            a = jnp.broadcast_to(h4x[y : y + 1, :], (8, 128))
            b = jnp.broadcast_to(hx[y : y + 1, :], (8, 128))
            r = jnp.broadcast_to(rx[y : y + 1, :], (8, 128))
            field[(x - 3) * 10 + j] = (a * u0[x, y] + b * w) * r
        return carry

    lax.fori_loop(3, 13, step, 0)

    for x in range(10):
        k_out[x * 10 : x * 10 + 10, :] = kk[x + 3, 3:13, :]
        e_out[x * 10 : x * 10 + 10, :] = ee[x + 3, 3:13, :]
        row = x * 10
        if 1 <= x < 9:
            c_out[row : row + 1, :] = ylow[36, x - 1 : x, :]
            c_out[row + 1 : row + 9, :] = padded[(x - 1) * 8 : (x - 1) * 8 + 8, :]
            c_out[row + 9 : row + 10, :] = yhigh[36, x - 1 : x, :]
        else:
            side, corner = (xlow, clow) if x == 0 else (xhigh, chigh)
            c_out[row : row + 1, :] = corner[36, 0:1, :]
            c_out[row + 1 : row + 9, :] = side[36]
            c_out[row + 9 : row + 10, :] = corner[36, 1:2, :]
    k_out[100:104, :] = jnp.zeros((4, 128), F32)
    e_out[100:104, :] = jnp.zeros((4, 128), F32)
    c_out[100:104, :] = jnp.full((4, 128), -1.0, F32)


def halves(t):
    first = t.astype(BF16)
    return first, (t - first.astype(F32)).astype(BF16)


def product(a, b):
    return lax.dot_general(a, b, (((1,), (0,)), ((), ())), preferred_element_type=F32)


def product_t(a, b):
    return lax.dot_general(a, b, (((1,), (1,)), ((), ())), preferred_element_type=F32)


def gather_lanes(t, index):
    return jnp.take_along_axis(t, index, axis=1)


def galerkin_kernel(
    vert, own, other, k10, e10, onehot, index,
    interp, coarse,
    rights, lhs_rows, r1s, r2s, e1s, e2s,
):
    first = vert[0] == 0
    lane16 = iota((16, 128), 1)
    sub16 = iota((16, 128), 0)
    lane8 = iota((8, 128), 1)
    sub8 = iota((8, 128), 0)
    block16, block8 = lane16 // 16, lane8 // 16
    lane128, sub128 = iota((128, 128), 1), iota((128, 128), 0)
    own_block = (lane128 % 64) // 8 == sub128 // 16
    ones = jnp.where(lane128 // 16 == sub128 // 16, 1.0, 0.0).astype(BF16)
    block_ones = [jnp.where(block16 == bb, 1.0, 0.0).astype(BF16) for bb in range(8)]
    on_diag = lane16 % 16 == sub16
    low128, high128 = z_weights(128)
    systems = []
    for g in range(13):
        n = 8 if g < 12 else 4
        a = own[8 * g : 8 * g + n].reshape(n * 8, 128)
        b = other[8 * g : 8 * g + n].reshape(n * 8, 128)
        fa, fb = jnp.where(first, a, b), jnp.where(first, b, a)
        if n == 8:
            f = jnp.concatenate([fa, fb], axis=0)
        else:
            none = jnp.zeros((32, 128), F32)
            f = jnp.concatenate([fa, none, fb, none], axis=0)
        f1, f2 = halves(f)
        oh = onehot[128 * g : 128 * g + 128, :]
        c1 = jnp.where(own_block, product_t(oh, f1), 0.0).astype(BF16)
        c2 = jnp.where(own_block, product_t(oh, f2), 0.0).astype(BF16)
        right = product(
            jnp.concatenate([c1, c1, c2], axis=1), jnp.concatenate([f1, f2, f1], axis=0)
        )
        rights[128 * g : 128 * g + 128, :] = right
        spots = jnp.broadcast_to(index[g : g + 1, :], (16, 128))
        wanted = jnp.maximum(spots, 0)
        gram = jnp.zeros((16, 128), F32)
        for bb in range(8):
            part = gather_lanes(right[16 * bb : 16 * bb + 16, :], wanted)
            gram = jnp.where(block16 == bb, part, gram)
        gram = jnp.where(spots >= 0, gram, 0.0)
        d = jnp.where(on_diag, gram, 0.0)
        d = d[0:8, :] + d[8:16, :]
        for shift in (4, 2, 1):
            d = d + pltpu.roll(d, shift, 0)
        for bit in (1, 2, 4, 8):
            d = d + gather_lanes(d, lane8 ^ bit)
        ridge = (RIDGE / 16) * d + 1e-06
        ridge = jnp.concatenate([ridge, ridge], axis=0)
        system = gram + jnp.where(on_diag, ridge, 0.0)
        systems.append([system[0:8, :], system[8:16, :]])

    for k in range(16):
        half, row = k // 8, k % 8
        at_k = lane8 % 16 == k
        spot = block8 * 16 + k
        for s in systems:
            pivot_row = jnp.broadcast_to(s[half][row : row + 1, :], (8, 128))
            scale = 1.0 / gather_lanes(pivot_row, spot)
            r = jnp.where(at_k, 1.0, pivot_row) * scale
            for t in range(2):
                factor = gather_lanes(s[t], spot)
                new = jnp.where(at_k, 0.0, s[t]) - factor * r
                if t == half:
                    new = jnp.where(sub8 == row, r, new)
                s[t] = new

    for g in range(13):
        m1, m2 = halves(jnp.concatenate(systems[g], axis=0))
        m1 = jnp.concatenate([m1 * block_ones[bb] for bb in range(8)], axis=0)
        m2 = jnp.concatenate([m2 * block_ones[bb] for bb in range(8)], axis=0)
        r1, r2 = halves(rights[128 * g : 128 * g + 128, :])
        w = product(
            jnp.concatenate([m1, m1, m2], axis=1), jnp.concatenate([r1, r2, r1], axis=0)
        )
        oh = onehot[128 * g : 128 * g + 128, :]
        c_row = product(ones, oh)
        p = w * (1.0 - c_row) + oh.astype(F32)
        kb = jnp.concatenate(
            [jnp.broadcast_to(k10[8 * g + bb : 8 * g + bb + 1, :], (16, 128)) for bb in range(8)],
            axis=0,
        )
        eb = jnp.concatenate(
            [jnp.broadcast_to(e10[8 * g + bb : 8 * g + bb + 1, :], (16, 128)) for bb in range(8)],
            axis=0,
        )
        left = kb * p
        image = along_z(left, low128, high128)
        centre = eb * p - image
        r1s[128 * g : 128 * g + 128, :], r2s[128 * g : 128 * g + 128, :] = halves(image)
        e1s[128 * g : 128 * g + 128, :], e2s[128 * g : 128 * g + 128, :] = halves(centre)
        for bb in range(8):
            x, y = divmod(8 * g + bb, 10)
            if 1 <= x < 9 and 1 <= y < 9:
                interp[(x - 1) * 8 + y - 1] = p[16 * bb : 16 * bb + 16, :]
                lhs_rows[x - 1, pl.ds(y - 1, 16, stride=8), :] = left[16 * bb : 16 * bb + 16, :]

    picks = [16 * ((sub8 + o) % 8) + lane8 % 16 for o in range(3)]
    for x in range(1, 9):
        l1, l2 = halves(lhs_rows[x - 1])
        lhs = jnp.concatenate([l1, l1, l2], axis=1)
        for ox in range(-1, 2):
            base = (x + ox) * 160

            def turned(ref):
                return jnp.concatenate(
                    [
                        ref[base : base + 160, :],
                        ref[base + 32 : base + 128, :],
                    ],
                    axis=0,
                )

            q1, q2 = turned(r1s), turned(r2s)
            t = product_t(lhs, jnp.concatenate([q1, q2, q1], axis=1))
            t0, t1 = t[:, 0:128], t[:, 128:256]
            if ox == 0:
                s1 = e1s[base + 16 : base + 144, :]
                s2 = e2s[base + 16 : base + 144, :]
                mid = product_t(lhs, jnp.concatenate([s1, s2, s1], axis=1))
            out = [[jnp.zeros((8, 128), F32) for half in range(2)] for oy in range(3)]
            for i in range(16):
                rows = slice(8 * i, 8 * i + 8)
                if ox == 0:
                    centre = gather_lanes(mid[rows, :], picks[0])
                else:
                    centre = gather_lanes(
                        jnp.where(block8 == 0, t1[rows, :], t0[rows, :]), picks[1]
                    )
                found = (
                    gather_lanes(t0[rows, :], picks[0]),
                    centre,
                    gather_lanes(t1[rows, :], picks[2]),
                )
                for oy in range(3):
                    out[oy][i // 8] = jnp.where(block8 == i % 8, found[oy], out[oy][i // 8])
            for oy in range(3):
                o = 3 * (ox + 1) + oy
                scale = 1.0 if o == 4 else (-1.0 if oy == 1 else -WY)
                for half in range(2):
                    coarse[x - 1, o, :, half * 128 : half * 128 + 128] = scale * out[oy][half]


def call(kernel, outs, scratch=(), specs=None, args=(), flops=0):
    shapes = [jax.ShapeDtypeStruct(*o) for o in outs]
    moved = sum(a.size * 4 for a in args) + sum(4 * s.size for s in shapes)
    return pl.pallas_call(
        kernel,
        out_shape=shapes,
        in_specs=specs or [pl.BlockSpec(memory_space=VMEM)] * len(args),
        out_specs=[pl.BlockSpec(memory_space=VMEM)] * len(outs),
        scratch_shapes=list(scratch),
        compiler_params=pltpu.CompilerParams(vmem_limit_bytes=48 << 20),
        cost_estimate=pl.CostEstimate(flops=flops, bytes_accessed=moved, transcendentals=0),
    )(*args)


def shifted(value, axis, step):
    count = lax.axis_size(axis)
    pairs = [(i, i + step) for i in range(count) if 0 <= i + step < count]
    return lax.ppermute(value, axis, pairs)


def body(vectors, conductivity, c_points):
    cond = conductivity.reshape(64, 128)
    tiles, ylow, yhigh, xlow, xhigh, padded = call(
        pack_kernel,
        [((64, 8, 128), F32)] + [(SLAB, F32)] * 4 + [((64, 128), F32)],
        args=(vectors.reshape(512, 128), cond, c_points.reshape(64, 16)),
    )
    from_ylow = shifted(yhigh, "gy", 1)
    from_yhigh = shifted(ylow, "gy", -1)
    from_xlow = shifted(xhigh, "gx", 1)
    from_xhigh = shifted(xlow, "gx", -1)
    clow, chigh = call(corner_kernel, [(SLAB, F32)] * 2, args=(from_ylow, from_yhigh))
    from_clow = shifted(chigh, "gx", 1)
    from_chigh = shifted(clow, "gx", -1)
    rows = ((104, 128), F32)
    field, k10, e10, c10 = call(
        sweep_kernel,
        [((100, 8, 128), F32), rows, rows, rows],
        [VMEM((16, 16, 8, 128), F32)] * 2 + [VMEM((16, 16, 128), F32)] * 6,
        args=(tiles, cond, padded, from_ylow, from_yhigh, from_xlow, from_xhigh, from_clow, from_chigh),
    )
    other = lax.ppermute(field, "vert", [(0, 1), (1, 0)])
    points = c10[:, 0:16].astype(jnp.int32)
    onehot = (points.reshape(1664, 1) == jnp.arange(128, dtype=jnp.int32)).astype(BF16)
    index = jnp.pad(points.reshape(13, 128), ((0, 3), (0, 0)))
    vert = lax.axis_index("vert").astype(jnp.int32).reshape(1)
    interp, coarse = call(
        galerkin_kernel,
        [((64, 16, 128), F32), ((8, 9, 8, 256), F32)],
        [VMEM((1664, 128), F32), VMEM((8, 128, 128), F32)] + [VMEM((1664, 128), BF16)] * 4,
        specs=[pl.BlockSpec(memory_space=pltpu.SMEM)] + [pl.BlockSpec(memory_space=VMEM)] * 6,
        args=(vert, field, other, k10, e10, onehot, index),
    )
    return interp.reshape(8, 8, 16, 128), jnp.transpose(coarse, (0, 2, 1, 3))


def solution(mesh):
    placed = (P("vert", "gx", "gy", None), P("gx", "gy", None), P("gx", "gy", None))
    return jax.shard_map(
        body,
        mesh=mesh,
        in_specs=placed,
        out_specs=(P("gx", "gy", None, None), P("gx", "gy", None, None)),
        check_vma=False,
    )
```

```python
import jax
import jax.numpy as jnp
from jax import lax
from jax.experimental import pallas as pl
from jax.experimental.pallas import tpu as pltpu
from jax.sharding import PartitionSpec as P


WY = 0.6
WZ = 0.15
OMEGA = 0.6
SHIFT = 0.5
RIDGE = 0.1
F32 = jnp.float32
BF16 = jnp.bfloat16
VMEM = pltpu.VMEM
SLAB = (37, 8, 128)
CROSS = (74, 8, 128)
SMEM = pl.BlockSpec(memory_space=pltpu.SMEM)
LOCAL = pl.BlockSpec(memory_space=VMEM)
BATCHES = ((0, 1, 2, 3), (4, 5, 6, 7), (8, 9, 10), (11, 12))
FAR = pl.BlockSpec(memory_space=pltpu.HBM)


def iota(shape, dim):
    return lax.broadcasted_iota(jnp.int32, shape, dim)


def along_z(t, low, high):
    return t + low * pltpu.roll(t, 1, 1) + high * pltpu.roll(t, 127, 1)


def z_weights(rows):
    lane = iota((rows, 128), 1)
    return jnp.where(lane == 0, 0.0, WZ), jnp.where(lane == 127, 0.0, WZ)


def pack_kernel(side, vec_in, cond_in, points_in, tiles, cond, padded, first, second, vec, points, sems):
    copies = [
        pltpu.make_async_copy(src, dst, sems.at[n])
        for n, (src, dst) in enumerate(
            ((vec_in, vec), (cond_in, cond), (points_in, points))
        )
    ]
    for copy in copies:
        copy.start()
    even = side[0]
    copies[2].wait()
    padded[...] = jnp.full((64, 128), -1.0, F32)
    padded[:, 0:16] = points[...].astype(F32)
    copies[1].wait()
    for out, up in ((first, even == 1), (second, even == 0)):
        for x in range(8):
            half = x % 2 * 4
            out[32 + x // 2, half : half + 4, :] = jnp.where(up, cond[x, 4:8, :], cond[x, 0:4, :])
        out[36] = jnp.where(up, padded[pl.ds(7, 8, stride=8), :], padded[pl.ds(0, 8, stride=8), :])
    copies[0].wait()
    for x in range(8):
        row = [vec[pl.ds(x * 8 + y, 8, stride=64), :] for y in range(8)]
        for y in range(8):
            tiles[x * 8 + y] = row[y]
        for y in range(4):
            first[x * 4 + y] = jnp.where(even == 1, row[y + 4], row[y])
            second[x * 4 + y] = jnp.where(even == 1, row[y], row[y + 4])


def cross_kernel(side, tiles, cond, padded, got1, got2, first, second):
    y_even, x_even = side[0] == 1, side[1]

    def low(*at):
        return jnp.where(y_even, got2[at], got1[at])

    def high(*at):
        return jnp.where(y_even, got1[at], got2[at])

    for out, up in ((first, x_even), (second, 1 - x_even)):
        for xx in range(4):
            x = xx + 4 * up
            for y in range(4):
                out[xx * 16 + y] = low(x * 4 + y)
                out[xx * 16 + 12 + y] = high(x * 4 + y)
            for y in range(8):
                out[xx * 16 + 4 + y] = tiles[x * 8 + y]
            rows = slice(xx % 2 * 4, xx % 2 * 4 + 4)
            k = cond[x]
            out[64 + 2 * xx, 0:4, :] = low(32 + xx // 2 + 2 * up, rows)
            out[64 + 2 * xx, 4:8, :] = k[0:4, :]
            out[65 + 2 * xx, 0:4, :] = k[4:8, :]
            out[65 + 2 * xx, 4:8, :] = high(32 + xx // 2 + 2 * up, rows)
        top = up == 1
        out[73] = jnp.zeros((8, 128), F32)
        out[72, 0:1, :] = jnp.where(top, low(36, slice(7, 8)), low(36, slice(0, 1)))
        out[72, 1:8, :] = jnp.where(top, padded[56:63, :], padded[0:7, :])
        out[73, 0:1, :] = jnp.where(top, padded[63:64, :], padded[7:8, :])
        out[73, 1:2, :] = jnp.where(top, high(36, slice(7, 8)), high(36, slice(0, 1)))


def sweep_kernel(
    side, tiles, cond, padded, got1, got2, cross1, cross2,
    field, k_out, e_out, c_out,
    u0, u1, kk, kz, hh, h4, rk, ee,
):
    y_even, x_even = side[0] == 1, side[1] == 1

    def ylow(*at):
        return jnp.where(y_even, got2[at], got1[at])

    def yhigh(*at):
        return jnp.where(y_even, got1[at], got2[at])

    def xlow(*at):
        return jnp.where(x_even, cross2[at], cross1[at])

    def xhigh(*at):
        return jnp.where(x_even, cross1[at], cross2[at])

    for x in range(16):
        if 4 <= x < 12:
            rows = slice(x % 2 * 4, x % 2 * 4 + 4)
            kk[x, 0:4, :] = ylow(32 + (x - 4) // 2, rows)
            kk[x, 4:12, :] = cond[x - 4]
            kk[x, 12:16, :] = yhigh(32 + (x - 4) // 2, rows)
        else:
            source, xx = (xlow, x) if x < 4 else (xhigh, x - 12)
            kk[x, 0:8, :] = source(64 + 2 * xx)
            kk[x, 8:16, :] = source(65 + 2 * xx)

    low16, high16 = z_weights(16)
    for x in range(16):
        kz[x] = along_z(kk[x], low16, high16)
    for x in range(1, 15):
        k = kk[x]
        s = kz[x - 1] + kz[x] + kz[x + 1]
        s = s + WY * (pltpu.roll(s, 1, 0) + pltpu.roll(s, 15, 0)) - k
        alive = k > 0.0
        h = jnp.where(alive, OMEGA * k / jnp.where(alive, SHIFT * k + s, 1.0), 0.0)
        hh[x] = h
        h4[x] = (1.0 - OMEGA) - h
        rk[x] = jnp.where(alive, 1.0 / jnp.where(alive, k, 1.0), 0.0)
        ee[x] = (SHIFT + 1.0) * k + s

    for x in range(16):
        for y in range(16):
            if x < 4:
                t = xlow(x * 16 + y)
            elif x >= 12:
                t = xhigh((x - 12) * 16 + y)
            elif y < 4:
                t = ylow((x - 4) * 4 + y)
            elif y >= 12:
                t = yhigh((x - 4) * 4 + y - 12)
            else:
                t = tiles[(x - 4) * 8 + y - 4]
            u0[x, y] = t * jnp.broadcast_to(kk[x, y : y + 1, :], (8, 128))

    low8, high8 = z_weights(8)

    def sweep(src, first, count, write):
        def step(x, carry):
            hx, h4x = hh[x], h4[x]
            s = [
                src[x - 1, y] + src[x, y] + src[x + 1, y]
                for y in range(first - 1, first + count + 1)
            ]
            for j in range(count):
                y = first + j
                t = s[j + 1] + WY * (s[j] + s[j + 2])
                w = along_z(t, low8, high8)
                a = jnp.broadcast_to(h4x[y : y + 1, :], (8, 128))
                b = jnp.broadcast_to(hx[y : y + 1, :], (8, 128))
                write(x, y, a * src[x, y] + b * w)
            return carry

        lax.fori_loop(first, first + count, step, 0, unroll=2)

    def to_u1(x, y, value):
        u1[x, y] = value

    def to_u0(x, y, value):
        u0[x, y] = value

    sweep(u0, 1, 14, to_u1)
    sweep(u1, 2, 12, to_u0)

    def step(x, carry):
        hx, h4x, rx = hh[x], h4[x], rk[x]
        s = [u0[x - 1, y] + u0[x, y] + u0[x + 1, y] for y in range(2, 14)]
        for j in range(10):
            y = 3 + j
            t = s[j + 1] + WY * (s[j] + s[j + 2])
            w = along_z(t, low8, high8)
            a = jnp.broadcast_to(h4x[y : y + 1, :], (8, 128))
            b = jnp.broadcast_to(hx[y : y + 1, :], (8, 128))
            r = jnp.broadcast_to(rx[y : y + 1, :], (8, 128))
            field[(x - 3) * 10 + j] = (a * u0[x, y] + b * w) * r
        return carry

    lax.fori_loop(3, 13, step, 0, unroll=2)

    for x in range(10):
        k_out[x * 10 : x * 10 + 10, :] = kk[x + 3, 3:13, :]
        e_out[x * 10 : x * 10 + 10, :] = ee[x + 3, 3:13, :]
        row = x * 10
        if 1 <= x < 9:
            c_out[row : row + 1, :] = ylow(36, slice(x - 1, x))
            c_out[row + 1 : row + 9, :] = padded[(x - 1) * 8 : (x - 1) * 8 + 8, :]
            c_out[row + 9 : row + 10, :] = yhigh(36, slice(x - 1, x))
        else:
            source = xlow if x == 0 else xhigh
            c_out[row : row + 8, :] = source(72)
            c_out[row + 8 : row + 10, :] = source(73, slice(0, 2))
    k_out[100:104, :] = jnp.zeros((4, 128), F32)
    e_out[100:104, :] = jnp.zeros((4, 128), F32)
    c_out[100:104, :] = jnp.full((4, 128), -1.0, F32)


def halves(t):
    first = t.astype(BF16)
    return first, (t - first.astype(F32)).astype(BF16)


def product(a, b):
    return lax.dot_general(a, b, (((1,), (0,)), ((), ())), preferred_element_type=F32)


def product_t(a, b):
    return lax.dot_general(a, b, (((1,), (1,)), ((), ())), preferred_element_type=F32)


def gather_lanes(t, index):
    return jnp.take_along_axis(t, index, axis=1)


def galerkin_kernel(
    vert, own, other, k10, e10, onehot, index,
    interp, coarse,
    rs, ps, l1s, l2s, r1s, r2s, e1s, e2s, ts, mids, cs, sems,
):
    first = vert[0] == 0
    lane16 = iota((16, 128), 1)
    sub16 = iota((16, 128), 0)
    lane8 = iota((8, 128), 1)
    sub8 = iota((8, 128), 0)
    block16, block8 = lane16 // 16, lane8 // 16
    lane128, sub128 = iota((128, 128), 1), iota((128, 128), 0)
    own_block = (lane128 % 64) // 8 == sub128 // 16
    ones = jnp.where(lane128 // 16 == sub128 // 16, 1.0, 0.0).astype(BF16)
    block_ones = [jnp.where(block16 == bb, 1.0, 0.0).astype(BF16) for bb in range(8)]
    on_diag = lane16 % 16 == sub16
    low128, high128 = z_weights(128)

    def rows_of(g):
        return slice(128 * g, 128 * g + 128)

    def fields(g):
        n = 8 if g < 12 else 4
        a = own[8 * g : 8 * g + n].reshape(n * 8, 128)
        b = other[8 * g : 8 * g + n].reshape(n * 8, 128)
        fa, fb = jnp.where(first, a, b), jnp.where(first, b, a)
        if n == 8:
            return halves(jnp.concatenate([fa, fb], axis=0))
        none = jnp.zeros((32, 128), F32)
        return halves(jnp.concatenate([fa, none, fb, none], axis=0))

    def values(g, pair):
        oh = onehot[rows_of(g), :]
        return [jnp.where(own_block, product_t(oh, f), 0.0).astype(BF16) for f in pair]

    def rights(pair, spots):
        f1, f2 = pair
        c1, c2 = spots
        return product(
            jnp.concatenate([c1, c1, c2], axis=1), jnp.concatenate([f1, f2, f1], axis=0)
        )

    def system_of(g, right):
        spots = jnp.broadcast_to(index[g : g + 1, :], (16, 128))
        wanted = jnp.maximum(spots, 0)
        gram = jnp.zeros((16, 128), F32)
        for bb in range(8):
            part = gather_lanes(right[16 * bb : 16 * bb + 16, :], wanted)
            gram = jnp.where(block16 == bb, part, gram)
        gram = jnp.where(spots >= 0, gram, 0.0)
        d = jnp.where(on_diag, gram, 0.0)
        d = d[0:8, :] + d[8:16, :]
        for shift in (4, 2, 1):
            d = d + pltpu.roll(d, shift, 0)
        for bit in (1, 2, 4, 8):
            d = d + gather_lanes(d, lane8 ^ bit)
        ridge = (RIDGE / 16) * d + 1e-06
        ridge = jnp.concatenate([ridge, ridge], axis=0)
        system = gram + jnp.where(on_diag, ridge, 0.0)
        return [system[0:8, :], system[8:16, :]]

    systems = []
    for batch in BATCHES:
        pairs = [fields(g) for g in batch]
        spots = [values(g, pair) for g, pair in zip(batch, pairs)]
        found = [rights(pair, spot) for pair, spot in zip(pairs, spots)]
        for g, right in zip(batch, found):
            rs[rows_of(g), :] = right
        systems += [system_of(g, right) for g, right in zip(batch, found)]

    for k in range(16):
        half, row = k // 8, k % 8
        at_k = lane8 % 16 == k
        spot = block8 * 16 + k
        for s in systems:
            pivot_row = jnp.broadcast_to(s[half][row : row + 1, :], (8, 128))
            scale = 1.0 / gather_lanes(pivot_row, spot)
            r = jnp.where(at_k, 1.0, pivot_row) * scale
            for t in range(2):
                factor = gather_lanes(s[t], spot)
                new = jnp.where(at_k, 0.0, s[t]) - factor * r
                if t == half:
                    new = jnp.where(sub8 == row, r, new)
                s[t] = new

    def weights(g):
        m1, m2 = halves(jnp.concatenate(systems[g], axis=0))
        m1 = jnp.concatenate([m1 * block_ones[bb] for bb in range(8)], axis=0)
        m2 = jnp.concatenate([m2 * block_ones[bb] for bb in range(8)], axis=0)
        r1, r2 = halves(rs[rows_of(g), :])
        w = product(
            jnp.concatenate([m1, m1, m2], axis=1), jnp.concatenate([r1, r2, r1], axis=0)
        )
        return w, product(ones, onehot[rows_of(g), :])

    def spread(ref, g):
        return jnp.concatenate(
            [jnp.broadcast_to(ref[8 * g + bb : 8 * g + bb + 1, :], (16, 128)) for bb in range(8)],
            axis=0,
        )

    def finish(g, w, c_row):
        p = w * (1.0 - c_row) + onehot[rows_of(g), :].astype(F32)
        ps[rows_of(g), :] = p
        left = spread(k10, g) * p
        padded = slice(128 * g + 160, 128 * g + 288)
        l1s[padded, :], l2s[padded, :] = halves(left)
        image = along_z(left, low128, high128)
        r1s[rows_of(g), :], r2s[rows_of(g), :] = halves(image)
        e1s[rows_of(g), :], e2s[rows_of(g), :] = halves(spread(e10, g) * p - image)

    for batch in BATCHES:
        found = [weights(g) for g in batch]
        for g, pair in zip(batch, found):
            finish(g, *pair)

    interp_copies = [
        pltpu.make_async_copy(
            ps.at[pl.ds((x * 10 + 1) * 16, 128), :], interp.at[pl.ds((x - 1) * 128, 128), :],
            sems.at[x - 1],
        )
        for x in range(1, 9)
    ]
    for copy in interp_copies:
        copy.start()

    def multiply(x, slot):
        base = x * 160
        low, high = max(x - 1, 1), min(x + 1, 8)

        def lefts(ref):
            return [ref[160 * n + 176 : 160 * n + 304, :] for n in range(low, high + 1)]

        def stacked(ref, order):
            return jnp.concatenate(
                [ref[base + 16 * y : base + 16 * y + 16, :] for y in order], axis=0
            )

        lhs = jnp.concatenate(
            [jnp.concatenate([a, a, b], axis=1) for a, b in zip(lefts(l1s), lefts(l2s))], axis=0
        )
        order = (0, 7, 6, 5, 4, 3, 2, 1, 8, 7, 6, 5, 4, 3, 2, 9)
        q1, q2 = stacked(r1s, order), stacked(r2s, order)
        at = 128 * (low - x + 1)
        ts[slot, at : at + 128 * (high - low + 1), :] = product_t(
            lhs, jnp.concatenate([q1, q2, q1], axis=1)
        )
        if 1 <= x <= 8:
            order = (8, 7, 6, 5, 4, 3, 2, 1)
            q1, q2 = stacked(e1s, order), stacked(e2s, order)
            at = 128 * (x - low)
            mids[slot] = product_t(lhs[at : at + 128, :], jnp.concatenate([q1, q2, q1], axis=1))

    def arrange(x, slot):
        for side in range(3):
            ox = 1 - side
            if not 1 <= x - ox <= 8:
                continue
            for o in range(3):
                first_turn, last_turn = min(o, 1), max(o - 1, 0)
                amount = (first_turn - o - block8) % 8
                scale = 1.0 if ox == 0 and o == 1 else (-1.0 if o == 1 else -WY)
                for half in range(2):
                    merged = jnp.zeros((8, 128), F32)
                    for y in range(8):
                        rows = slice(16 * y + 8 * half, 16 * y + 8 * half + 8)
                        if ox == 0 and o == 1:
                            part = mids[slot, rows, :]
                        else:
                            rows = slice(128 * side + rows.start, 128 * side + rows.stop)
                            if o == 2 or (o == 1 and y == 7):
                                part = ts[slot, rows, 128:256]
                            else:
                                part = ts[slot, rows, 0:128]
                        merged = jnp.where(block8 == (-y - o) % 8, part, merged)
                    merged = pltpu.roll(merged, 16 * first_turn, 1, stride=16, stride_axis=0)
                    for bit in (1, 2, 4):
                        merged = jnp.where(amount & bit != 0, pltpu.roll(merged, bit, 0), merged)
                    merged = pltpu.roll(merged, 16 * last_turn, 1, stride=16, stride_axis=0)
                    cs[x - ox - 1, 3 * (ox + 1) + o, :, half * 128 : half * 128 + 128] = scale * merged

    coarse_copies = [
        pltpu.make_async_copy(cs.at[x], coarse.at[x], sems.at[8 + x]) for x in range(8)
    ]
    multiply(0, 0)
    for x in range(1, 11):
        if x < 10:
            multiply(x, x % 2)
        arrange(x - 1, (x - 1) % 2)
        if x > 2:
            coarse_copies[x - 3].start()
    for copy in interp_copies:
        copy.wait()
    for copy in coarse_copies:
        copy.wait()


def call(kernel, outs, scratch=(), specs=None, args=(), flops=0, outs_at=LOCAL):
    shapes = [jax.ShapeDtypeStruct(*o) for o in outs]
    moved = sum(a.size * 4 for a in args) + sum(4 * s.size for s in shapes)
    return pl.pallas_call(
        kernel,
        out_shape=shapes,
        in_specs=specs,
        out_specs=[outs_at] * len(outs),
        scratch_shapes=list(scratch),
        compiler_params=pltpu.CompilerParams(vmem_limit_bytes=48 << 20),
        cost_estimate=pl.CostEstimate(flops=flops, bytes_accessed=moved, transcendentals=0),
    )(*args)


def swapped(value, axis, first):
    count = lax.axis_size(axis)
    low = [(i, i + 1) for i in range(first, count - 1, 2)]
    return lax.ppermute(value, axis, low + [(j, i) for i, j in low])


def body(vectors, conductivity, c_points):
    side = jnp.stack([1 - lax.axis_index("gy") % 2, 1 - lax.axis_index("gx") % 2]).astype(jnp.int32)
    tiles, cond, padded, send1, send2 = call(
        pack_kernel,
        [((64, 8, 128), F32), ((8, 8, 128), F32), ((64, 128), F32), (SLAB, F32), (SLAB, F32)],
        [VMEM((512, 128), F32), VMEM((64, 16), jnp.int32), pltpu.SemaphoreType.DMA((3,))],
        specs=[SMEM] + [FAR] * 3,
        args=(side, vectors.reshape(512, 128), conductivity, c_points.reshape(64, 16)),
    )
    got2 = swapped(send2, "gy", 1)
    got1 = swapped(send1, "gy", 0)
    send1, send2 = call(
        cross_kernel,
        [(CROSS, F32)] * 2,
        specs=[SMEM] + [LOCAL] * 5,
        args=(side, tiles, cond, padded, got1, got2),
    )
    cross2 = swapped(send2, "gx", 1)
    cross1 = swapped(send1, "gx", 0)
    rows = ((104, 128), F32)
    field, k10, e10, c10 = call(
        sweep_kernel,
        [((100, 8, 128), F32), rows, rows, rows],
        [VMEM((16, 16, 8, 128), F32)] * 2 + [VMEM((16, 16, 128), F32)] * 6,
        specs=[SMEM] + [LOCAL] * 7,
        args=(side, tiles, cond, padded, got1, got2, cross1, cross2),
    )
    other = lax.ppermute(field, "vert", [(0, 1), (1, 0)])
    points = c10[:, 0:16].astype(jnp.int32)
    onehot = (points.reshape(1664, 1) == jnp.arange(128, dtype=jnp.int32)).astype(BF16)
    index = jnp.pad(points.reshape(13, 128), ((0, 3), (0, 0)))
    vert = lax.axis_index("vert").astype(jnp.int32).reshape(1)
    strips = [VMEM((1664, 128), F32)] * 2 + [VMEM((1920, 128), BF16)] * 2 + [VMEM((1664, 128), BF16)] * 4
    interp, coarse = call(
        galerkin_kernel,
        [((1024, 128), F32), ((8, 9, 8, 256), F32)],
        strips
        + [VMEM((2, 384, 256), F32), VMEM((2, 128, 128), F32), VMEM((8, 9, 8, 256), F32)]
        + [pltpu.SemaphoreType.DMA((16,))],
        specs=[SMEM] + [LOCAL] * 6,
        outs_at=FAR,
        args=(vert, field, other, k10, e10, onehot, index),
    )
    return interp.reshape(8, 8, 16, 128), jnp.transpose(coarse, (0, 2, 1, 3))


def solution(mesh):
    placed = (P("vert", "gx", "gy", None), P("gx", "gy", None), P("gx", "gy", None))
    return jax.shard_map(
        body,
        mesh=mesh,
        in_specs=placed,
        out_specs=(P("gx", "gy", None, None), P("gx", "gy", None, None)),
        check_vma=False,
    )
```

```python
import jax
import jax.numpy as jnp
from jax import lax
from jax.experimental import pallas as pl
from jax.experimental.pallas import tpu as pltpu
from jax.sharding import PartitionSpec as P


WY = 0.6
WZ = 0.15
OMEGA = 0.6
SHIFT = 0.5
RIDGE = 0.1
F32 = jnp.float32
BF16 = jnp.bfloat16
VMEM = pltpu.VMEM
SLAB = (37, 8, 128)
CROSS = (74, 8, 128)
LOCAL = pl.BlockSpec(memory_space=VMEM)
BATCHES = (((0, 1, 2, 3), (4, 5, 6, 7)), ((8, 9, 10), (11, 12)))
FAR = pl.BlockSpec(memory_space=pltpu.HBM)


def iota(shape, dim):
    return lax.broadcasted_iota(jnp.int32, shape, dim)


def along_z(t, low, high):
    return t + low * pltpu.roll(t, 1, 1) + high * pltpu.roll(t, 127, 1)


def z_weights(rows):
    lane = iota((rows, 128), 1)
    return jnp.where(lane == 0, 0.0, WZ), jnp.where(lane == 127, 0.0, WZ)


def pack_kernel(tiles, cond, points, padded, first, second):
    even = 1 - lax.axis_index("gy") % 2
    padded[...] = jnp.full((64, 128), -1.0, F32)
    padded[:, 0:16] = points[...].astype(F32)
    for out, up in ((first, even), (second, 1 - even)):
        for x in range(8):
            half = x % 2 * 4
            out[32 + x // 2, half : half + 4, :] = jnp.where(up == 1, cond[x, 4:8, :], cond[x, 0:4, :])
            for y in range(4):
                out[x * 4 + y] = tiles[x * 8 + y + 4 * up]
        ends = padded[pl.ds(0, 8, stride=8), :], padded[pl.ds(7, 8, stride=8), :]
        out[36] = jnp.where(up == 1, ends[1], ends[0])


def cross_kernel(tiles, cond, padded, got1, got2, first, second):
    y_even, x_even = lax.axis_index("gy") % 2 == 0, 1 - lax.axis_index("gx") % 2

    def low(*at):
        return jnp.where(y_even, got2[at], got1[at])

    def high(*at):
        return jnp.where(y_even, got1[at], got2[at])

    for out, up in ((first, x_even), (second, 1 - x_even)):
        for xx in range(4):
            x = xx + 4 * up
            for y in range(4):
                out[xx * 16 + y] = low(x * 4 + y)
                out[xx * 16 + 12 + y] = high(x * 4 + y)
            for y in range(8):
                out[xx * 16 + 4 + y] = tiles[x * 8 + y]
            rows = slice(xx % 2 * 4, xx % 2 * 4 + 4)
            k = cond[x]
            out[64 + 2 * xx, 0:4, :] = low(32 + xx // 2 + 2 * up, rows)
            out[64 + 2 * xx, 4:8, :] = k[0:4, :]
            out[65 + 2 * xx, 0:4, :] = k[4:8, :]
            out[65 + 2 * xx, 4:8, :] = high(32 + xx // 2 + 2 * up, rows)
        top = up == 1
        out[73] = jnp.zeros((8, 128), F32)
        out[72, 0:1, :] = jnp.where(top, low(36, slice(7, 8)), low(36, slice(0, 1)))
        out[72, 1:8, :] = jnp.where(top, padded[56:63, :], padded[0:7, :])
        out[73, 0:1, :] = jnp.where(top, padded[63:64, :], padded[7:8, :])
        out[73, 1:2, :] = jnp.where(top, high(36, slice(7, 8)), high(36, slice(0, 1)))


def sweep_kernel(
    tiles, cond, padded, got1, got2, cross1, cross2,
    field_a, field_b, k_out, e_out, c_out,
    u0, u1, kk, kz, hh, h4, rk, ee,
):
    y_even, x_even = lax.axis_index("gy") % 2 == 0, lax.axis_index("gx") % 2 == 0

    def ylow(*at):
        return jnp.where(y_even, got2[at], got1[at])

    def yhigh(*at):
        return jnp.where(y_even, got1[at], got2[at])

    def xlow(*at):
        return jnp.where(x_even, cross2[at], cross1[at])

    def xhigh(*at):
        return jnp.where(x_even, cross1[at], cross2[at])

    for x in range(16):
        if 4 <= x < 12:
            rows = slice(x % 2 * 4, x % 2 * 4 + 4)
            kk[x, 0:4, :] = ylow(32 + (x - 4) // 2, rows)
            kk[x, 4:12, :] = cond[x - 4]
            kk[x, 12:16, :] = yhigh(32 + (x - 4) // 2, rows)
        else:
            source, xx = (xlow, x) if x < 4 else (xhigh, x - 12)
            kk[x, 0:8, :] = source(64 + 2 * xx)
            kk[x, 8:16, :] = source(65 + 2 * xx)

    low16, high16 = z_weights(16)
    for x in range(16):
        kz[x] = along_z(kk[x], low16, high16)
    for x in range(1, 15):
        k = kk[x]
        s = kz[x - 1] + kz[x] + kz[x + 1]
        s = s + WY * (pltpu.roll(s, 1, 0) + pltpu.roll(s, 15, 0)) - k
        alive = k > 0.0
        h = jnp.where(alive, OMEGA * k / jnp.where(alive, SHIFT * k + s, 1.0), 0.0)
        hh[x] = h
        h4[x] = (1.0 - OMEGA) - h
        rk[x] = jnp.where(alive, 1.0 / jnp.where(alive, k, 1.0), 0.0)
        ee[x] = (SHIFT + 1.0) * k + s

    for x in range(16):
        for y in range(16):
            if x < 4:
                t = xlow(x * 16 + y)
            elif x >= 12:
                t = xhigh((x - 12) * 16 + y)
            elif y < 4:
                t = ylow((x - 4) * 4 + y)
            elif y >= 12:
                t = yhigh((x - 4) * 4 + y - 12)
            else:
                t = tiles[(x - 4) * 8 + y - 4]
            u0[x, y] = t * jnp.broadcast_to(kk[x, y : y + 1, :], (8, 128))

    low8, high8 = z_weights(8)

    def sweep(src, first, count, write):
        def step(x, carry):
            hx, h4x = hh[x], h4[x]
            s = [
                src[x - 1, y] + src[x, y] + src[x + 1, y]
                for y in range(first - 1, first + count + 1)
            ]
            for j in range(count):
                y = first + j
                t = s[j + 1] + WY * (s[j] + s[j + 2])
                w = along_z(t, low8, high8)
                a = jnp.broadcast_to(h4x[y : y + 1, :], (8, 128))
                b = jnp.broadcast_to(hx[y : y + 1, :], (8, 128))
                write(x, y, a * src[x, y] + b * w)
            return carry

        lax.fori_loop(first, first + count, step, 0, unroll=count)

    def to_u1(x, y, value):
        u1[x, y] = value

    def to_u0(x, y, value):
        u0[x, y] = value

    sweep(u0, 1, 14, to_u1)
    sweep(u1, 2, 12, to_u0)

    def last(x, write):
        hx, h4x, rx = hh[x], h4[x], rk[x]
        s = [u0[x - 1, y] + u0[x, y] + u0[x + 1, y] for y in range(2, 14)]
        for j in range(10):
            y = 3 + j
            t = s[j + 1] + WY * (s[j] + s[j + 2])
            w = along_z(t, low8, high8)
            a = jnp.broadcast_to(h4x[y : y + 1, :], (8, 128))
            b = jnp.broadcast_to(hx[y : y + 1, :], (8, 128))
            r = jnp.broadcast_to(rx[y : y + 1, :], (8, 128))
            write(j, (a * u0[x, y] + b * w) * r)

    def low_rows(x, carry):
        def write(j, value):
            field_a[(x - 3) * 10 + j] = value

        last(x, write)
        return carry

    def high_rows(x, carry):
        def write(j, value):
            field_b[(x - 3) * 10 + j - 64] = value

        last(x, write)
        return carry

    def middle(j, value):
        if j < 4:
            field_a[60 + j] = value
        else:
            field_b[j - 4] = value

    lax.fori_loop(3, 9, low_rows, 0, unroll=6)
    last(9, middle)
    lax.fori_loop(10, 13, high_rows, 0, unroll=3)

    for x in range(10):
        k_out[x * 10 : x * 10 + 10, :] = kk[x + 3, 3:13, :]
        e_out[x * 10 : x * 10 + 10, :] = ee[x + 3, 3:13, :]
        row = x * 10
        if 1 <= x < 9:
            c_out[row : row + 1, :] = ylow(36, slice(x - 1, x))
            c_out[row + 1 : row + 9, :] = padded[(x - 1) * 8 : (x - 1) * 8 + 8, :]
            c_out[row + 9 : row + 10, :] = yhigh(36, slice(x - 1, x))
        else:
            source = xlow if x == 0 else xhigh
            c_out[row : row + 8, :] = source(72)
            c_out[row + 8 : row + 10, :] = source(73, slice(0, 2))
    k_out[100:104, :] = jnp.zeros((4, 128), F32)
    e_out[100:104, :] = jnp.zeros((4, 128), F32)
    c_out[100:104, :] = jnp.full((4, 128), -1.0, F32)


def halves(t):
    first = t.astype(BF16)
    return first, (t - first.astype(F32)).astype(BF16)


def product(a, b):
    return lax.dot_general(a, b, (((1,), (0,)), ((), ())), preferred_element_type=F32)


def product_t(a, b):
    return lax.dot_general(a, b, (((1,), (1,)), ((), ())), preferred_element_type=F32)


def gather_lanes(t, index):
    return jnp.take_along_axis(t, index, axis=1)


KEPT = slice(800, 1024)


def early_kernel(*refs):
    galerkin(0, refs[:6], (), refs[6:8], refs[8:14], refs[14:])


def late_kernel(*refs):
    galerkin(1, refs[:6], refs[6:14], refs[14:16], (), refs[16:])


def galerkin(part, sources, given, outputs, kept, scratch):
    own, other, k10, e10, onehot, index = sources
    if part == 0:
        ps, cs = outputs
        rs, l1s, l2s, r1s, r2s, e1s, e2s, ts, mids = scratch
    else:
        interp, coarse = outputs
        rs, l1s, l2s, r1s, r2s, e1s, e2s, ts, mids, ps, cs, sems = scratch
        early_ps, early_cs = given[0], given[1]

    def interp_copy(x, source):
        return pltpu.make_async_copy(
            source.at[pl.ds((x * 10 + 1) * 16, 128), :],
            interp.at[pl.ds((x - 1) * 128, 128), :],
            sems.at[x - 1],
        )

    def coarse_copy(x, source):
        return pltpu.make_async_copy(source.at[x - 1], coarse.at[x - 1], sems.at[7 + x])

    copies = []
    if part == 1:
        copies += [interp_copy(x, early_ps) for x in range(1, 6)]
        copies += [coarse_copy(x, early_cs) for x in range(1, 5)]
        for copy in copies:
            copy.start()
    groups = range(8) if part == 0 else range(8, 13)
    first = lax.axis_index("vert") == 0
    lane16 = iota((16, 128), 1)
    sub16 = iota((16, 128), 0)
    lane8 = iota((8, 128), 1)
    sub8 = iota((8, 128), 0)
    block16, block8 = lane16 // 16, lane8 // 16
    lane128, sub128 = iota((128, 128), 1), iota((128, 128), 0)
    own_block = (lane128 % 64) // 8 == sub128 // 16
    ones = jnp.where(lane128 // 16 == sub128 // 16, 1.0, 0.0).astype(BF16)
    block_ones = [jnp.where(block16 == bb, 1.0, 0.0).astype(BF16) for bb in range(8)]
    on_diag = lane16 % 16 == sub16
    low128, high128 = z_weights(128)

    def rows_of(g):
        return slice(128 * g, 128 * g + 128)

    def fields(g):
        n = 8 if g < 12 else 4
        at = slice(8 * (g - groups[0]), 8 * (g - groups[0]) + n)
        a = own[at].reshape(n * 8, 128)
        b = other[at].reshape(n * 8, 128)
        fa, fb = jnp.where(first, a, b), jnp.where(first, b, a)
        if n == 8:
            return halves(jnp.concatenate([fa, fb], axis=0))
        none = jnp.zeros((32, 128), F32)
        return halves(jnp.concatenate([fa, none, fb, none], axis=0))

    def values(g, pair):
        oh = onehot[rows_of(g), :]
        return [jnp.where(own_block, product_t(oh, f), 0.0).astype(BF16) for f in pair]

    def rights(pair, spots):
        f1, f2 = pair
        c1, c2 = spots
        return product(
            jnp.concatenate([c1, c1, c2], axis=1), jnp.concatenate([f1, f2, f1], axis=0)
        )

    def system_of(g, right):
        spots = jnp.broadcast_to(index[g : g + 1, :], (16, 128))
        wanted = jnp.maximum(spots, 0)
        gram = jnp.zeros((16, 128), F32)
        for bb in range(8):
            part = gather_lanes(right[16 * bb : 16 * bb + 16, :], wanted)
            gram = jnp.where(block16 == bb, part, gram)
        gram = jnp.where(spots >= 0, gram, 0.0)
        d = jnp.where(on_diag, gram, 0.0)
        d = d[0:8, :] + d[8:16, :]
        for shift in (4, 2, 1):
            d = d + pltpu.roll(d, shift, 0)
        for bit in (1, 2, 4, 8):
            d = d + gather_lanes(d, lane8 ^ bit)
        ridge = (RIDGE / 16) * d + 1e-06
        ridge = jnp.concatenate([ridge, ridge], axis=0)
        system = gram + jnp.where(on_diag, ridge, 0.0)
        return [system[0:8, :], system[8:16, :]]

    systems = {}
    for batch in BATCHES[part]:
        pairs = [fields(g) for g in batch]
        spots = [values(g, pair) for g, pair in zip(batch, pairs)]
        found = [rights(pair, spot) for pair, spot in zip(pairs, spots)]
        for g, right in zip(batch, found):
            rs[rows_of(g), :] = right
        systems.update({g: system_of(g, right) for g, right in zip(batch, found)})

    for k in range(0, 16, 2):
        half, row = k // 8, k % 8
        at_0, at_1 = lane8 % 16 == k, lane8 % 16 == k + 1
        spot = block8 * 16 + k

        def row_of(t, row):
            return jnp.broadcast_to(t[row : row + 1, :], (8, 128))

        for s in systems.values():
            f0 = [gather_lanes(t, spot) for t in s]
            f1 = [gather_lanes(t, spot + 1) for t in s]
            a, b, c = row_of(f0[half], row), row_of(f1[half], row), row_of(f1[half], row + 1)
            inverse = 1.0 / (a * c - b * b)
            p0, p1 = row_of(s[half], row), row_of(s[half], row + 1)
            p0 = jnp.where(at_0, 1.0, jnp.where(at_1, 0.0, p0))
            p1 = jnp.where(at_1, 1.0, jnp.where(at_0, 0.0, p1))
            r0, r1 = (c * p0 - b * p1) * inverse, (a * p1 - b * p0) * inverse
            for t in range(2):
                new = jnp.where(at_0 | at_1, 0.0, s[t]) - f0[t] * r0 - f1[t] * r1
                if t == half:
                    new = jnp.where(sub8 == row, r0, jnp.where(sub8 == row + 1, r1, new))
                s[t] = new

    def weights(g):
        m1, m2 = halves(jnp.concatenate(systems[g], axis=0))
        m1 = jnp.concatenate([m1 * block_ones[bb] for bb in range(8)], axis=0)
        m2 = jnp.concatenate([m2 * block_ones[bb] for bb in range(8)], axis=0)
        r1, r2 = halves(rs[rows_of(g), :])
        w = product(
            jnp.concatenate([m1, m1, m2], axis=1), jnp.concatenate([r1, r2, r1], axis=0)
        )
        return w, product(ones, onehot[rows_of(g), :])

    def spread(ref, g):
        return jnp.concatenate(
            [jnp.broadcast_to(ref[8 * g + bb : 8 * g + bb + 1, :], (16, 128)) for bb in range(8)],
            axis=0,
        )

    def finish(g, w, c_row):
        p = w * (1.0 - c_row) + onehot[rows_of(g), :].astype(F32)
        ps[rows_of(g), :] = p
        left = spread(k10, g) * p
        padded = slice(128 * g + 160, 128 * g + 288)
        l1s[padded, :], l2s[padded, :] = halves(left)
        image = along_z(left, low128, high128)
        r1s[rows_of(g), :], r2s[rows_of(g), :] = halves(image)
        e1s[rows_of(g), :], e2s[rows_of(g), :] = halves(spread(e10, g) * p - image)

    for batch in BATCHES[part]:
        found = [weights(g) for g in batch]
        for g, pair in zip(batch, found):
            finish(g, *pair)

    moved = slice(KEPT.start + 160, KEPT.stop + 160)
    pieces = ((l1s, moved), (l2s, moved), (r1s, KEPT), (r2s, KEPT), (e1s, KEPT), (e2s, KEPT))
    if part == 0:
        for to, (ref, at) in zip(kept, pieces):
            to[...] = ref[at, :]
    else:
        for source, (ref, at) in zip(given[2:], pieces):
            ref[at, :] = source[...]
        ps[KEPT, :] = early_ps[KEPT, :]
        cs[4, 0:6] = early_cs[4, 0:6]
        late_copies = [interp_copy(x, ps) for x in range(6, 9)]
        for copy in late_copies:
            copy.start()
        copies += late_copies

    def wanted(x, source):
        return 1 <= x <= 8 and (max(x, source) <= 5) == (part == 0)

    def multiply(x, slot):
        base = x * 160
        used = [n for n in range(x - 1, x + 2) if wanted(n, x)]
        low, high = used[0], used[-1]

        def lefts(ref):
            return [ref[160 * n + 176 : 160 * n + 304, :] for n in range(low, high + 1)]

        def stacked(ref, order):
            return jnp.concatenate(
                [ref[base + 16 * y : base + 16 * y + 16, :] for y in order], axis=0
            )

        lhs = jnp.concatenate(
            [jnp.concatenate([a, a, b], axis=1) for a, b in zip(lefts(l1s), lefts(l2s))], axis=0
        )
        order = (0, 7, 6, 5, 4, 3, 2, 1, 8, 7, 6, 5, 4, 3, 2, 9)
        q1, q2 = stacked(r1s, order), stacked(r2s, order)
        at = 128 * (low - x + 1)
        ts[slot, at : at + 128 * (high - low + 1), :] = product_t(
            lhs, jnp.concatenate([q1, q2, q1], axis=1)
        )
        if wanted(x, x):
            order = (8, 7, 6, 5, 4, 3, 2, 1)
            q1, q2 = stacked(e1s, order), stacked(e2s, order)
            at = 128 * (x - low)
            mids[slot] = product_t(lhs[at : at + 128, :], jnp.concatenate([q1, q2, q1], axis=1))

    def arrange(x, slot):
        for side in range(3):
            ox = 1 - side
            if not wanted(x - ox, x):
                continue
            for o in range(3):
                first_turn, last_turn = min(o, 1), max(o - 1, 0)
                amount = (first_turn - o - block8) % 8
                scale = 1.0 if ox == 0 and o == 1 else (-1.0 if o == 1 else -WY)
                for half in range(2):
                    merged = jnp.zeros((8, 128), F32)
                    for y in range(8):
                        rows = slice(16 * y + 8 * half, 16 * y + 8 * half + 8)
                        if ox == 0 and o == 1:
                            part = mids[slot, rows, :]
                        else:
                            rows = slice(128 * side + rows.start, 128 * side + rows.stop)
                            if o == 2 or (o == 1 and y == 7):
                                part = ts[slot, rows, 128:256]
                            else:
                                part = ts[slot, rows, 0:128]
                        merged = jnp.where(block8 == (-y - o) % 8, part, merged)
                    merged = pltpu.roll(merged, 16 * first_turn, 1, stride=16, stride_axis=0)
                    for bit in (1, 2, 4):
                        merged = jnp.where(amount & bit != 0, pltpu.roll(merged, bit, 0), merged)
                    merged = pltpu.roll(merged, 16 * last_turn, 1, stride=16, stride_axis=0)
                    cs[x - ox - 1, 3 * (ox + 1) + o, :, half * 128 : half * 128 + 128] = scale * merged

    order = range(6) if part == 0 else range(5, 10)
    multiply(order[0], 0)
    for n, x in enumerate(order):
        if n + 1 < len(order):
            multiply(x + 1, (n + 1) % 2)
        arrange(x, n % 2)
        if part == 1 and x > 5:
            copies.append(coarse_copy(x - 1, cs))
            copies[-1].start()
    for copy in copies:
        copy.wait()


def call(kernel, outs, scratch=(), specs=None, args=(), flops=0, outs_at=None):
    shapes = [jax.ShapeDtypeStruct(*o) for o in outs]
    moved = sum(a.size * 4 for a in args) + sum(4 * s.size for s in shapes)
    return pl.pallas_call(
        kernel,
        out_shape=shapes,
        in_specs=specs or [LOCAL] * len(args),
        out_specs=outs_at or [LOCAL] * len(outs),
        scratch_shapes=list(scratch),
        compiler_params=pltpu.CompilerParams(vmem_limit_bytes=48 << 20),
        cost_estimate=pl.CostEstimate(flops=flops, bytes_accessed=moved, transcendentals=0),
    )(*args)


def swapped(value, axis, first):
    count = lax.axis_size(axis)
    low = [(i, i + 1) for i in range(first, count - 1, 2)]
    return lax.ppermute(value, axis, low + [(j, i) for i, j in low])


def body(vectors, conductivity, c_points):
    tiles = jnp.transpose(vectors, (1, 2, 0, 3)).reshape(64, 8, 128)
    padded, send1, send2 = call(
        pack_kernel,
        [((64, 128), F32), (SLAB, F32), (SLAB, F32)],
        args=(tiles, conductivity, c_points.reshape(64, 16)),
    )
    cond = conductivity
    got2 = swapped(send2, "gy", 1)
    got1 = swapped(send1, "gy", 0)
    send1, send2 = call(
        cross_kernel,
        [(CROSS, F32)] * 2,
        args=(tiles, cond, padded, got1, got2),
    )
    cross2 = swapped(send2, "gx", 1)
    cross1 = swapped(send1, "gx", 0)
    rows = ((104, 128), F32)
    field_a, field_b, k10, e10, c10 = call(
        sweep_kernel,
        [((64, 8, 128), F32), ((36, 8, 128), F32), rows, rows, rows],
        [VMEM((16, 16, 8, 128), F32)] * 2 + [VMEM((16, 16, 128), F32)] * 6,
        args=(tiles, cond, padded, got1, got2, cross1, cross2),
    )
    pair = [(0, 1), (1, 0)]
    other_a = lax.ppermute(field_a, "vert", pair)
    other_b = lax.ppermute(field_b, "vert", pair)
    points = c10[:, 0:16].astype(jnp.int32)
    onehot = (points.reshape(1664, 1) == jnp.arange(128, dtype=jnp.int32)).astype(BF16)
    index = jnp.pad(points.reshape(13, 128), ((0, 3), (0, 0)))
    scratch = (
        [VMEM((1664, 128), F32)] + [VMEM((1920, 128), BF16)] * 2 + [VMEM((1664, 128), BF16)] * 4
        + [VMEM((2, 384, 256), F32), VMEM((2, 128, 128), F32)]
    )
    late_scratch = [
        VMEM((1664, 128), F32), VMEM((8, 9, 8, 256), F32), pltpu.SemaphoreType.DMA((16,)),
    ]
    kept = [((1024, 128), F32), ((5, 9, 8, 256), F32)] + [((224, 128), BF16)] * 6
    kept = call(
        early_kernel, kept, scratch, args=(field_a, other_a, k10, e10, onehot, index)
    )
    interp, coarse = call(
        late_kernel,
        [((1024, 128), F32), ((8, 9, 8, 256), F32)],
        scratch + late_scratch,
        outs_at=[FAR] * 2,
        args=(field_b, other_b, k10, e10, onehot, index, *kept),
    )
    return interp.reshape(8, 8, 16, 128), jnp.transpose(coarse, (0, 2, 1, 3))


def solution(mesh):
    placed = (P("vert", "gx", "gy", None), P("gx", "gy", None), P("gx", "gy", None))
    return jax.shard_map(
        body,
        mesh=mesh,
        in_specs=placed,
        out_specs=(P("gx", "gy", None, None), P("gx", "gy", None, None)),
        check_vma=False,
    )
```

```python
import jax
import jax.numpy as jnp
from jax import lax
from jax.experimental import pallas as pl
from jax.experimental.pallas import tpu as pltpu
from jax.sharding import PartitionSpec as P


WY = 0.6
WZ = 0.15
OMEGA = 0.6
SHIFT = 0.5
RIDGE = 0.1
F32 = jnp.float32
BF16 = jnp.bfloat16
VMEM = pltpu.VMEM
SLAB = (37, 8, 128)
CROSS = (74, 8, 128)
LOCAL = pl.BlockSpec(memory_space=VMEM)
BATCHES = (((0, 1, 2, 3), (4, 5, 6, 7)), ((8, 9, 10), (11, 12)))
FAR = pl.BlockSpec(memory_space=pltpu.HBM)


def iota(shape, dim):
    return lax.broadcasted_iota(jnp.int32, shape, dim)


def along_z(t, low, high):
    return t + low * pltpu.roll(t, 1, 1) + high * pltpu.roll(t, 127, 1)


def z_weights(rows):
    lane = iota((rows, 128), 1)
    return jnp.where(lane == 0, 0.0, WZ), jnp.where(lane == 127, 0.0, WZ)


def pack_kernel(tiles, cond, points, padded, first, second, beside):
    even = 1 - lax.axis_index("gy") % 2
    padded[...] = jnp.full((64, 128), -1.0, F32)
    padded[:, 0:16] = points[...].astype(F32)
    for out, up in ((first, even), (second, 1 - even)):
        for x in range(8):
            half = x % 2 * 4
            out[32 + x // 2, half : half + 4, :] = jnp.where(up == 1, cond[x, 4:8, :], cond[x, 0:4, :])
            for y in range(4):
                out[x * 4 + y] = tiles[x * 8 + y + 4 * up]
        ends = padded[pl.ds(0, 8, stride=8), :], padded[pl.ds(7, 8, stride=8), :]
        out[36] = jnp.where(up == 1, ends[1], ends[0])
    own_part(beside, 0, lax.axis_index("gx") % 2, tiles, cond, padded)


def own_part(out, start, up, tiles, cond, padded):
    for x in range(4):
        for y in range(8):
            out[start + x * 8 + y] = tiles[(x + 4 * up) * 8 + y]
        out[start + 32 + x] = cond[x + 4 * up]
    out[start + 36] = jnp.where(up == 1, padded[56:64, :], padded[0:8, :])


def middle_kernel(tiles, cond, padded, first):
    own_part(first, 0, 1 - lax.axis_index("gx") % 2, tiles, cond, padded)


def cross_kernel(filled, got1, got2, first, second):
    y_even, up = lax.axis_index("gy") % 2 == 0, lax.axis_index("gx") % 2

    def low(*at):
        return jnp.where(y_even, got2[at], got1[at])

    def high(*at):
        return jnp.where(y_even, got1[at], got2[at])

    for out, start, up in ((first, 37, 1 - up), (second, 0, up)):
        for x in range(4):
            for y in range(4):
                out[start + x * 8 + y] = low((x + 4 * up) * 4 + y)
                out[start + x * 8 + 4 + y] = high((x + 4 * up) * 4 + y)
            rows = slice(x % 2 * 4, x % 2 * 4 + 4)
            out[start + 32 + x, 0:4, :] = low(32 + x // 2 + 2 * up, rows)
            out[start + 32 + x, 4:8, :] = high(32 + x // 2 + 2 * up, rows)
        out[start + 36] = jnp.zeros((8, 128), F32)
        for row, source in ((0, low), (1, high)):
            out[start + 36, row : row + 1, :] = jnp.where(
                up == 1, source(36, slice(7, 8)), source(36, slice(0, 1))
            )


def sweep_kernel(
    tiles, cond, padded, got1, got2, near, far_own, far_corner,
    field_a, field_b, k_out, e_out, c_out,
    u0, u1, kk, kz, hh, h4, rk, ee,
):
    y_even, x_even = lax.axis_index("gy") % 2 == 0, lax.axis_index("gx") % 2 == 0

    def ylow(*at):
        return jnp.where(y_even, got2[at], got1[at])

    def yhigh(*at):
        return jnp.where(y_even, got1[at], got2[at])

    def own(is_low, *at):
        a, b = far_own[at], near[at]
        return jnp.where(x_even, a, b) if is_low else jnp.where(x_even, b, a)

    def corner(is_low, n, *at):
        a, b = far_corner[(n, *at)], near[(n + 37, *at)]
        return jnp.where(x_even, a, b) if is_low else jnp.where(x_even, b, a)

    for x in range(16):
        if 4 <= x < 12:
            rows = slice(x % 2 * 4, x % 2 * 4 + 4)
            kk[x, 0:4, :] = ylow(32 + (x - 4) // 2, rows)
            kk[x, 4:12, :] = cond[x - 4]
            kk[x, 12:16, :] = yhigh(32 + (x - 4) // 2, rows)
        else:
            n = 32 + x % 4
            kk[x, 0:4, :] = corner(x < 4, n, slice(0, 4))
            kk[x, 4:12, :] = own(x < 4, n)
            kk[x, 12:16, :] = corner(x < 4, n, slice(4, 8))

    low16, high16 = z_weights(16)
    for x in range(16):
        kz[x] = along_z(kk[x], low16, high16)
    for x in range(1, 15):
        k = kk[x]
        s = kz[x - 1] + kz[x] + kz[x + 1]
        s = s + WY * (pltpu.roll(s, 1, 0) + pltpu.roll(s, 15, 0)) - k
        alive = k > 0.0
        h = jnp.where(alive, OMEGA * k / jnp.where(alive, SHIFT * k + s, 1.0), 0.0)
        hh[x] = h
        h4[x] = (1.0 - OMEGA) - h
        rk[x] = jnp.where(alive, 1.0 / jnp.where(alive, k, 1.0), 0.0)
        ee[x] = (SHIFT + 1.0) * k + s

    for x in range(16):
        for y in range(16):
            if not 4 <= x < 12:
                if 4 <= y < 12:
                    t = own(x < 4, x % 4 * 8 + y - 4)
                else:
                    t = corner(x < 4, x % 4 * 8 + (y if y < 4 else y - 8))
            elif y < 4:
                t = ylow((x - 4) * 4 + y)
            elif y >= 12:
                t = yhigh((x - 4) * 4 + y - 12)
            else:
                t = tiles[(x - 4) * 8 + y - 4]
            u0[x, y] = t * jnp.broadcast_to(kk[x, y : y + 1, :], (8, 128))

    low8, high8 = z_weights(8)

    def sweep(src, first, count, write):
        def step(x, carry):
            hx, h4x = hh[x], h4[x]
            s = [
                src[x - 1, y] + src[x, y] + src[x + 1, y]
                for y in range(first - 1, first + count + 1)
            ]
            for j in range(count):
                y = first + j
                t = s[j + 1] + WY * (s[j] + s[j + 2])
                w = along_z(t, low8, high8)
                a = jnp.broadcast_to(h4x[y : y + 1, :], (8, 128))
                b = jnp.broadcast_to(hx[y : y + 1, :], (8, 128))
                write(x, y, a * src[x, y] + b * w)
            return carry

        lax.fori_loop(first, first + count, step, 0, unroll=count)

    def to_u1(x, y, value):
        u1[x, y] = value

    def to_u0(x, y, value):
        u0[x, y] = value

    sweep(u0, 1, 14, to_u1)
    sweep(u1, 2, 12, to_u0)

    def last(x, write):
        hx, h4x, rx = hh[x], h4[x], rk[x]
        s = [u0[x - 1, y] + u0[x, y] + u0[x + 1, y] for y in range(2, 14)]
        for j in range(10):
            y = 3 + j
            t = s[j + 1] + WY * (s[j] + s[j + 2])
            w = along_z(t, low8, high8)
            a = jnp.broadcast_to(h4x[y : y + 1, :], (8, 128))
            b = jnp.broadcast_to(hx[y : y + 1, :], (8, 128))
            r = jnp.broadcast_to(rx[y : y + 1, :], (8, 128))
            write(j, (a * u0[x, y] + b * w) * r)

    def low_rows(x, carry):
        def write(j, value):
            field_a[(x - 3) * 10 + j] = value

        last(x, write)
        return carry

    def high_rows(x, carry):
        def write(j, value):
            field_b[(x - 3) * 10 + j - 64] = value

        last(x, write)
        return carry

    def middle(j, value):
        if j < 4:
            field_a[60 + j] = value
        else:
            field_b[j - 4] = value

    lax.fori_loop(3, 9, low_rows, 0, unroll=6)
    last(9, middle)
    lax.fori_loop(10, 13, high_rows, 0, unroll=3)

    for x in range(10):
        k_out[x * 10 : x * 10 + 10, :] = kk[x + 3, 3:13, :]
        e_out[x * 10 : x * 10 + 10, :] = ee[x + 3, 3:13, :]
        row = x * 10
        if 1 <= x < 9:
            c_out[row : row + 1, :] = ylow(36, slice(x - 1, x))
            c_out[row + 1 : row + 9, :] = padded[(x - 1) * 8 : (x - 1) * 8 + 8, :]
            c_out[row + 9 : row + 10, :] = yhigh(36, slice(x - 1, x))
        else:
            c_out[row : row + 1, :] = corner(x == 0, 36, slice(0, 1))
            c_out[row + 1 : row + 9, :] = own(x == 0, 36)
            c_out[row + 9 : row + 10, :] = corner(x == 0, 36, slice(1, 2))
    k_out[100:104, :] = jnp.zeros((4, 128), F32)
    e_out[100:104, :] = jnp.zeros((4, 128), F32)
    c_out[100:104, :] = jnp.full((4, 128), -1.0, F32)


def halves(t):
    first = t.astype(BF16)
    return first, (t - first.astype(F32)).astype(BF16)


def product(a, b):
    return lax.dot_general(a, b, (((1,), (0,)), ((), ())), preferred_element_type=F32)


def product_t(a, b):
    return lax.dot_general(a, b, (((1,), (1,)), ((), ())), preferred_element_type=F32)


def gather_lanes(t, index):
    return jnp.take_along_axis(t, index, axis=1)


KEPT = slice(800, 1024)


def early_kernel(*refs):
    galerkin(0, refs[:6], (), refs[6:8], refs[8:14], refs[14:])


def late_kernel(*refs):
    galerkin(1, refs[:6], refs[6:14], refs[14:16], (), refs[16:])


def galerkin(part, sources, given, outputs, kept, scratch):
    own, other, k10, e10, onehot, index = sources
    if part == 0:
        ps, cs = outputs
        rs, l1s, l2s, r1s, r2s, e1s, e2s, ts, mids = scratch
    else:
        interp, coarse = outputs
        rs, l1s, l2s, r1s, r2s, e1s, e2s, ts, mids, ps, cs, sems = scratch
        early_ps, early_cs = given[0], given[1]

    def interp_copy(x, source):
        return pltpu.make_async_copy(
            source.at[pl.ds((x * 10 + 1) * 16, 128), :],
            interp.at[pl.ds((x - 1) * 128, 128), :],
            sems.at[x - 1],
        )

    def coarse_copy(x, source):
        return pltpu.make_async_copy(source.at[x - 1], coarse.at[x - 1], sems.at[7 + x])

    copies = []
    if part == 1:
        copies += [interp_copy(x, early_ps) for x in range(1, 6)]
        copies += [coarse_copy(x, early_cs) for x in range(1, 5)]
        for copy in copies:
            copy.start()
    groups = range(8) if part == 0 else range(8, 13)
    first = lax.axis_index("vert") == 0
    lane16 = iota((16, 128), 1)
    sub16 = iota((16, 128), 0)
    lane8 = iota((8, 128), 1)
    sub8 = iota((8, 128), 0)
    block16, block8 = lane16 // 16, lane8 // 16
    lane128, sub128 = iota((128, 128), 1), iota((128, 128), 0)
    own_block = (lane128 % 64) // 8 == sub128 // 16
    ones = jnp.where(lane128 // 16 == sub128 // 16, 1.0, 0.0).astype(BF16)
    block_ones = [jnp.where(block16 == bb, 1.0, 0.0).astype(BF16) for bb in range(8)]
    on_diag = lane16 % 16 == sub16
    low128, high128 = z_weights(128)

    def rows_of(g):
        return slice(128 * g, 128 * g + 128)

    def fields(g):
        n = 8 if g < 12 else 4
        at = slice(8 * (g - groups[0]), 8 * (g - groups[0]) + n)
        a = own[at].reshape(n * 8, 128)
        b = other[at].reshape(n * 8, 128)
        fa, fb = jnp.where(first, a, b), jnp.where(first, b, a)
        if n == 8:
            return halves(jnp.concatenate([fa, fb], axis=0))
        none = jnp.zeros((32, 128), F32)
        return halves(jnp.concatenate([fa, none, fb, none], axis=0))

    def values(g, pair):
        oh = onehot[rows_of(g), :]
        return [jnp.where(own_block, product_t(oh, f), 0.0).astype(BF16) for f in pair]

    def rights(pair, spots):
        f1, f2 = pair
        c1, c2 = spots
        return product(
            jnp.concatenate([c1, c1, c2], axis=1), jnp.concatenate([f1, f2, f1], axis=0)
        )

    def system_of(g, right):
        spots = jnp.broadcast_to(index[g : g + 1, :], (16, 128))
        wanted = jnp.maximum(spots, 0)
        gram = jnp.zeros((16, 128), F32)
        for bb in range(8):
            part = gather_lanes(right[16 * bb : 16 * bb + 16, :], wanted)
            gram = jnp.where(block16 == bb, part, gram)
        gram = jnp.where(spots >= 0, gram, 0.0)
        d = jnp.where(on_diag, gram, 0.0)
        d = d[0:8, :] + d[8:16, :]
        for shift in (4, 2, 1):
            d = d + pltpu.roll(d, shift, 0)
        for bit in (1, 2, 4, 8):
            d = d + gather_lanes(d, lane8 ^ bit)
        ridge = (RIDGE / 16) * d + 1e-06
        ridge = jnp.concatenate([ridge, ridge], axis=0)
        system = gram + jnp.where(on_diag, ridge, 0.0)
        return [system[0:8, :], system[8:16, :]]

    systems = {}
    for batch in BATCHES[part]:
        pairs = [fields(g) for g in batch]
        spots = [values(g, pair) for g, pair in zip(batch, pairs)]
        found = [rights(pair, spot) for pair, spot in zip(pairs, spots)]
        for g, right in zip(batch, found):
            rs[rows_of(g), :] = right
        systems.update({g: system_of(g, right) for g, right in zip(batch, found)})

    for k in range(0, 16, 2):
        half, row = k // 8, k % 8
        at_0, at_1 = lane8 % 16 == k, lane8 % 16 == k + 1
        spot = block8 * 16 + k

        def row_of(t, row):
            return jnp.broadcast_to(t[row : row + 1, :], (8, 128))

        for s in systems.values():
            f0 = [gather_lanes(t, spot) for t in s]
            f1 = [gather_lanes(t, spot + 1) for t in s]
            a, b, c = row_of(f0[half], row), row_of(f1[half], row), row_of(f1[half], row + 1)
            inverse = 1.0 / (a * c - b * b)
            p0, p1 = row_of(s[half], row), row_of(s[half], row + 1)
            p0 = jnp.where(at_0, 1.0, jnp.where(at_1, 0.0, p0))
            p1 = jnp.where(at_1, 1.0, jnp.where(at_0, 0.0, p1))
            r0, r1 = (c * p0 - b * p1) * inverse, (a * p1 - b * p0) * inverse
            for t in range(2):
                new = jnp.where(at_0 | at_1, 0.0, s[t]) - f0[t] * r0 - f1[t] * r1
                if t == half:
                    new = jnp.where(sub8 == row, r0, jnp.where(sub8 == row + 1, r1, new))
                s[t] = new

    def weights(g):
        m1, m2 = halves(jnp.concatenate(systems[g], axis=0))
        m1 = jnp.concatenate([m1 * block_ones[bb] for bb in range(8)], axis=0)
        m2 = jnp.concatenate([m2 * block_ones[bb] for bb in range(8)], axis=0)
        r1, r2 = halves(rs[rows_of(g), :])
        w = product(
            jnp.concatenate([m1, m1, m2], axis=1), jnp.concatenate([r1, r2, r1], axis=0)
        )
        return w, product(ones, onehot[rows_of(g), :])

    def spread(ref, g):
        return jnp.concatenate(
            [jnp.broadcast_to(ref[8 * g + bb : 8 * g + bb + 1, :], (16, 128)) for bb in range(8)],
            axis=0,
        )

    def finish(g, w, c_row):
        p = w * (1.0 - c_row) + onehot[rows_of(g), :].astype(F32)
        ps[rows_of(g), :] = p
        left = spread(k10, g) * p
        padded = slice(128 * g + 160, 128 * g + 288)
        l1s[padded, :], l2s[padded, :] = halves(left)
        image = along_z(left, low128, high128)
        r1s[rows_of(g), :], r2s[rows_of(g), :] = halves(image)
        e1s[rows_of(g), :], e2s[rows_of(g), :] = halves(spread(e10, g) * p - image)

    for batch in BATCHES[part]:
        found = [weights(g) for g in batch]
        for g, pair in zip(batch, found):
            finish(g, *pair)

    moved = slice(KEPT.start + 160, KEPT.stop + 160)
    pieces = ((l1s, moved), (l2s, moved), (r1s, KEPT), (r2s, KEPT), (e1s, KEPT), (e2s, KEPT))
    if part == 0:
        for to, (ref, at) in zip(kept, pieces):
            to[...] = ref[at, :]
    else:
        for source, (ref, at) in zip(given[2:], pieces):
            ref[at, :] = source[...]
        ps[KEPT, :] = early_ps[KEPT, :]
        cs[4, 0:6] = early_cs[4, 0:6]
        late_copies = [interp_copy(x, ps) for x in range(6, 9)]
        for copy in late_copies:
            copy.start()
        copies += late_copies

    def wanted(x, source):
        return 1 <= x <= 8 and (max(x, source) <= 5) == (part == 0)

    def multiply(x, slot):
        base = x * 160
        used = [n for n in range(x - 1, x + 2) if wanted(n, x)]
        low, high = used[0], used[-1]

        def lefts(ref):
            return [ref[160 * n + 176 : 160 * n + 304, :] for n in range(low, high + 1)]

        def stacked(ref, order):
            return jnp.concatenate(
                [ref[base + 16 * y : base + 16 * y + 16, :] for y in order], axis=0
            )

        lhs = jnp.concatenate(
            [jnp.concatenate([a, a, b], axis=1) for a, b in zip(lefts(l1s), lefts(l2s))], axis=0
        )
        order = (0, 7, 6, 5, 4, 3, 2, 1, 8, 7, 6, 5, 4, 3, 2, 9)
        q1, q2 = stacked(r1s, order), stacked(r2s, order)
        at = 128 * (low - x + 1)
        ts[slot, at : at + 128 * (high - low + 1), :] = product_t(
            lhs, jnp.concatenate([q1, q2, q1], axis=1)
        )
        if wanted(x, x):
            order = (8, 7, 6, 5, 4, 3, 2, 1)
            q1, q2 = stacked(e1s, order), stacked(e2s, order)
            at = 128 * (x - low)
            mids[slot] = product_t(lhs[at : at + 128, :], jnp.concatenate([q1, q2, q1], axis=1))

    def arrange(x, slot):
        for side in range(3):
            ox = 1 - side
            if not wanted(x - ox, x):
                continue
            for o in range(3):
                first_turn, last_turn = min(o, 1), max(o - 1, 0)
                amount = (first_turn - o - block8) % 8
                scale = 1.0 if ox == 0 and o == 1 else (-1.0 if o == 1 else -WY)
                for half in range(2):
                    merged = jnp.zeros((8, 128), F32)
                    for y in range(8):
                        rows = slice(16 * y + 8 * half, 16 * y + 8 * half + 8)
                        if ox == 0 and o == 1:
                            part = mids[slot, rows, :]
                        else:
                            rows = slice(128 * side + rows.start, 128 * side + rows.stop)
                            if o == 2 or (o == 1 and y == 7):
                                part = ts[slot, rows, 128:256]
                            else:
                                part = ts[slot, rows, 0:128]
                        merged = jnp.where(block8 == (-y - o) % 8, part, merged)
                    merged = pltpu.roll(merged, 16 * first_turn, 1, stride=16, stride_axis=0)
                    for bit in (1, 2, 4):
                        merged = jnp.where(amount & bit != 0, pltpu.roll(merged, bit, 0), merged)
                    merged = pltpu.roll(merged, 16 * last_turn, 1, stride=16, stride_axis=0)
                    cs[x - ox - 1, 3 * (ox + 1) + o, :, half * 128 : half * 128 + 128] = scale * merged

    order = range(6) if part == 0 else range(5, 10)
    multiply(order[0], 0)
    for n, x in enumerate(order):
        if n + 1 < len(order):
            multiply(x + 1, (n + 1) % 2)
        arrange(x, n % 2)
        if part == 1 and x > 5:
            copies.append(coarse_copy(x - 1, cs))
            copies[-1].start()
    for copy in copies:
        copy.wait()


def call(kernel, outs, scratch=(), specs=None, args=(), flops=0, outs_at=None, aliases=None):
    shapes = [jax.ShapeDtypeStruct(*o) for o in outs]
    moved = sum(a.size * 4 for a in args) + sum(4 * s.size for s in shapes)
    return pl.pallas_call(
        kernel,
        out_shape=shapes,
        in_specs=specs or [LOCAL] * len(args),
        out_specs=outs_at or [LOCAL] * len(outs),
        scratch_shapes=list(scratch),
        input_output_aliases=aliases or {},
        compiler_params=pltpu.CompilerParams(vmem_limit_bytes=48 << 20),
        cost_estimate=pl.CostEstimate(flops=flops, bytes_accessed=moved, transcendentals=0),
    )(*args)


def swapped(value, axis, first):
    count = lax.axis_size(axis)
    low = [(i, i + 1) for i in range(first, count - 1, 2)]
    return lax.ppermute(value, axis, low + [(j, i) for i, j in low])


def body(vectors, conductivity, c_points):
    tiles = jnp.transpose(vectors, (1, 2, 0, 3)).reshape(64, 8, 128)
    cond = conductivity
    padded, send1, send2, beside = call(
        pack_kernel,
        [((64, 128), F32), (SLAB, F32), (SLAB, F32), (SLAB, F32)],
        args=(tiles, cond, c_points.reshape(64, 16)),
    )
    got2 = swapped(send2, "gy", 1)
    got1 = swapped(send1, "gy", 0)
    far_own = swapped(beside, "gx", 1)
    (filled,) = call(middle_kernel, [(CROSS, F32)], args=(tiles, cond, padded))
    send1, send2 = call(
        cross_kernel, [(CROSS, F32), (SLAB, F32)], args=(filled, got1, got2), aliases={0: 0}
    )
    far_corner = swapped(send2, "gx", 1)
    near = swapped(send1, "gx", 0)
    rows = ((104, 128), F32)
    field_a, field_b, k10, e10, c10 = call(
        sweep_kernel,
        [((64, 8, 128), F32), ((36, 8, 128), F32), rows, rows, rows],
        [VMEM((16, 16, 8, 128), F32)] * 2 + [VMEM((16, 16, 128), F32)] * 6,
        args=(tiles, cond, padded, got1, got2, near, far_own, far_corner),
    )
    pair = [(0, 1), (1, 0)]
    other_a = lax.ppermute(field_a, "vert", pair)
    other_b = lax.ppermute(field_b, "vert", pair)
    points = c10[:, 0:16].astype(jnp.int32)
    onehot = (points.reshape(1664, 1) == jnp.arange(128, dtype=jnp.int32)).astype(BF16)
    index = jnp.pad(points.reshape(13, 128), ((0, 3), (0, 0)))
    scratch = (
        [VMEM((1664, 128), F32)] + [VMEM((1920, 128), BF16)] * 2 + [VMEM((1664, 128), BF16)] * 4
        + [VMEM((2, 384, 256), F32), VMEM((2, 128, 128), F32)]
    )
    late_scratch = [
        VMEM((1664, 128), F32), VMEM((8, 9, 8, 256), F32), pltpu.SemaphoreType.DMA((16,)),
    ]
    kept = [((1024, 128), F32), ((5, 9, 8, 256), F32)] + [((224, 128), BF16)] * 6
    kept = call(
        early_kernel, kept, scratch, args=(field_a, other_a, k10, e10, onehot, index)
    )
    interp, coarse = call(
        late_kernel,
        [((1024, 128), F32), ((8, 9, 8, 256), F32)],
        scratch + late_scratch,
        outs_at=[FAR] * 2,
        args=(field_b, other_b, k10, e10, onehot, index, *kept),
    )
    return interp.reshape(8, 8, 16, 128), jnp.transpose(coarse, (0, 2, 1, 3))


def solution(mesh):
    placed = (P("vert", "gx", "gy", None), P("gx", "gy", None), P("gx", "gy", None))
    return jax.shard_map(
        body,
        mesh=mesh,
        in_specs=placed,
        out_specs=(P("gx", "gy", None, None), P("gx", "gy", None, None)),
        check_vma=False,
    )
```

```python
import jax
import jax.numpy as jnp
from jax import lax
from jax.experimental import pallas as pl
from jax.experimental.pallas import tpu as pltpu
from jax.sharding import PartitionSpec as P


WY = 0.6
WZ = 0.15
OMEGA = 0.6
SHIFT = 0.5
RIDGE = 0.1
F32 = jnp.float32
BF16 = jnp.bfloat16
VMEM = pltpu.VMEM
GROUPS = 7
COLUMNS = 8 * GROUPS
FULL = COLUMNS // 10
KEPT = slice(160 * (FULL - 1), 16 * COLUMNS)
SIZE = KEPT.stop - KEPT.start
SLAB = (37, 8, 128)
CROSS = (74, 8, 128)
LOCAL = pl.BlockSpec(memory_space=VMEM)
FAR = pl.BlockSpec(memory_space=pltpu.HBM)


def iota(shape, dim):
    return lax.broadcasted_iota(jnp.int32, shape, dim)


def along_z(t, low, high):
    return t + low * pltpu.roll(t, 1, 1) + high * pltpu.roll(t, 127, 1)


def z_weights(rows):
    lane = iota((rows, 128), 1)
    return jnp.where(lane == 0, 0.0, WZ), jnp.where(lane == 127, 0.0, WZ)


def pack_kernel(tiles, cond, points, padded, first, second, beside):
    even = 1 - lax.axis_index("gy") % 2
    padded[...] = jnp.full((64, 128), -1.0, F32)
    padded[:, 0:16] = points[...].astype(F32)
    for out, up in ((first, even), (second, 1 - even)):
        for x in range(8):
            half = x % 2 * 4
            out[32 + x // 2, half : half + 4, :] = jnp.where(up == 1, cond[x, 4:8, :], cond[x, 0:4, :])
            for y in range(4):
                out[x * 4 + y] = tiles[x * 8 + y + 4 * up]
        ends = padded[pl.ds(0, 8, stride=8), :], padded[pl.ds(7, 8, stride=8), :]
        out[36] = jnp.where(up == 1, ends[1], ends[0])
    own_part(beside, 0, lax.axis_index("gx") % 2, tiles, cond, padded)


def own_part(out, start, up, tiles, cond, padded):
    for x in range(4):
        for y in range(8):
            out[start + x * 8 + y] = tiles[(x + 4 * up) * 8 + y]
        out[start + 32 + x] = cond[x + 4 * up]
    out[start + 36] = jnp.where(up == 1, padded[56:64, :], padded[0:8, :])


def middle_kernel(tiles, cond, padded, first):
    own_part(first, 0, 1 - lax.axis_index("gx") % 2, tiles, cond, padded)


def cross_kernel(filled, got1, got2, first, second):
    y_even, up = lax.axis_index("gy") % 2 == 0, lax.axis_index("gx") % 2

    def low(*at):
        return jnp.where(y_even, got2[at], got1[at])

    def high(*at):
        return jnp.where(y_even, got1[at], got2[at])

    for out, start, up in ((first, 37, 1 - up), (second, 0, up)):
        for x in range(4):
            for y in range(4):
                out[start + x * 8 + y] = low((x + 4 * up) * 4 + y)
                out[start + x * 8 + 4 + y] = high((x + 4 * up) * 4 + y)
            rows = slice(x % 2 * 4, x % 2 * 4 + 4)
            out[start + 32 + x, 0:4, :] = low(32 + x // 2 + 2 * up, rows)
            out[start + 32 + x, 4:8, :] = high(32 + x // 2 + 2 * up, rows)
        out[start + 36] = jnp.zeros((8, 128), F32)
        for row, source in ((0, low), (1, high)):
            out[start + 36, row : row + 1, :] = jnp.where(
                up == 1, source(36, slice(7, 8)), source(36, slice(0, 1))
            )


def sweep_kernel(
    tiles, cond, padded, got1, got2, near, far_own, far_corner,
    field_a, field_b, k_out, e_out, c_out,
    u0, u1, kk, kz, hh, h4, rk, ee,
):
    y_even, x_even = lax.axis_index("gy") % 2 == 0, lax.axis_index("gx") % 2 == 0

    def ylow(*at):
        return jnp.where(y_even, got2[at], got1[at])

    def yhigh(*at):
        return jnp.where(y_even, got1[at], got2[at])

    def own(is_low, *at):
        a, b = far_own[at], near[at]
        return jnp.where(x_even, a, b) if is_low else jnp.where(x_even, b, a)

    def corner(is_low, n, *at):
        a, b = far_corner[(n, *at)], near[(n + 37, *at)]
        return jnp.where(x_even, a, b) if is_low else jnp.where(x_even, b, a)

    for x in range(16):
        if 4 <= x < 12:
            rows = slice(x % 2 * 4, x % 2 * 4 + 4)
            kk[x, 0:4, :] = ylow(32 + (x - 4) // 2, rows)
            kk[x, 4:12, :] = cond[x - 4]
            kk[x, 12:16, :] = yhigh(32 + (x - 4) // 2, rows)
        else:
            n = 32 + x % 4
            kk[x, 0:4, :] = corner(x < 4, n, slice(0, 4))
            kk[x, 4:12, :] = own(x < 4, n)
            kk[x, 12:16, :] = corner(x < 4, n, slice(4, 8))

    low16, high16 = z_weights(16)
    for x in range(16):
        kz[x] = along_z(kk[x], low16, high16)
    for x in range(1, 15):
        k = kk[x]
        s = kz[x - 1] + kz[x] + kz[x + 1]
        s = s + WY * (pltpu.roll(s, 1, 0) + pltpu.roll(s, 15, 0)) - k
        alive = k > 0.0
        h = jnp.where(alive, OMEGA * k / jnp.where(alive, SHIFT * k + s, 1.0), 0.0)
        hh[x] = h
        h4[x] = (1.0 - OMEGA) - h
        rk[x] = jnp.where(alive, 1.0 / jnp.where(alive, k, 1.0), 0.0)
        ee[x] = (SHIFT + 1.0) * k + s

    for x in range(16):
        for y in range(16):
            if not 4 <= x < 12:
                if 4 <= y < 12:
                    t = own(x < 4, x % 4 * 8 + y - 4)
                else:
                    t = corner(x < 4, x % 4 * 8 + (y if y < 4 else y - 8))
            elif y < 4:
                t = ylow((x - 4) * 4 + y)
            elif y >= 12:
                t = yhigh((x - 4) * 4 + y - 12)
            else:
                t = tiles[(x - 4) * 8 + y - 4]
            u0[x, y] = t * jnp.broadcast_to(kk[x, y : y + 1, :], (8, 128))

    low8, high8 = z_weights(8)

    def sweep(src, first, count, write):
        def step(x, carry):
            hx, h4x = hh[x], h4[x]
            s = [
                src[x - 1, y] + src[x, y] + src[x + 1, y]
                for y in range(first - 1, first + count + 1)
            ]
            for j in range(count):
                y = first + j
                t = s[j + 1] + WY * (s[j] + s[j + 2])
                w = along_z(t, low8, high8)
                a = jnp.broadcast_to(h4x[y : y + 1, :], (8, 128))
                b = jnp.broadcast_to(hx[y : y + 1, :], (8, 128))
                write(x, y, a * src[x, y] + b * w)
            return carry

        lax.fori_loop(first, first + count, step, 0, unroll=count)

    def to_u1(x, y, value):
        u1[x, y] = value

    def to_u0(x, y, value):
        u0[x, y] = value

    sweep(u0, 1, 14, to_u1)
    sweep(u1, 2, 12, to_u0)

    def last(x, write):
        hx, h4x, rx = hh[x], h4[x], rk[x]
        s = [u0[x - 1, y] + u0[x, y] + u0[x + 1, y] for y in range(2, 14)]
        for j in range(10):
            y = 3 + j
            t = s[j + 1] + WY * (s[j] + s[j + 2])
            w = along_z(t, low8, high8)
            a = jnp.broadcast_to(h4x[y : y + 1, :], (8, 128))
            b = jnp.broadcast_to(hx[y : y + 1, :], (8, 128))
            r = jnp.broadcast_to(rx[y : y + 1, :], (8, 128))
            write(j, (a * u0[x, y] + b * w) * r)

    for x in range(10):

        def write(j, value, x=x):
            column = x * 10 + j
            if column < COLUMNS:
                field_a[column] = value
            else:
                field_b[column - COLUMNS] = value

        last(x + 3, write)

    for x in range(10):
        k_out[x * 10 : x * 10 + 10, :] = kk[x + 3, 3:13, :]
        e_out[x * 10 : x * 10 + 10, :] = ee[x + 3, 3:13, :]
        row = x * 10
        if 1 <= x < 9:
            c_out[row : row + 1, :] = ylow(36, slice(x - 1, x))
            c_out[row + 1 : row + 9, :] = padded[(x - 1) * 8 : (x - 1) * 8 + 8, :]
            c_out[row + 9 : row + 10, :] = yhigh(36, slice(x - 1, x))
        else:
            c_out[row : row + 1, :] = corner(x == 0, 36, slice(0, 1))
            c_out[row + 1 : row + 9, :] = own(x == 0, 36)
            c_out[row + 9 : row + 10, :] = corner(x == 0, 36, slice(1, 2))
    k_out[100:104, :] = jnp.zeros((4, 128), F32)
    e_out[100:104, :] = jnp.zeros((4, 128), F32)
    c_out[100:104, :] = jnp.full((4, 128), -1.0, F32)


def halves(t):
    first = t.astype(BF16)
    return first, (t - first.astype(F32)).astype(BF16)


def product(a, b):
    return lax.dot_general(a, b, (((1,), (0,)), ((), ())), preferred_element_type=F32)


def product_t(a, b):
    return lax.dot_general(a, b, (((1,), (1,)), ((), ())), preferred_element_type=F32)


def gather_lanes(t, index):
    return jnp.take_along_axis(t, index, axis=1)


def early_kernel(*refs):
    galerkin(0, refs[:6], (), refs[6:8], refs[8:14], refs[14:])


def late_kernel(*refs):
    galerkin(1, refs[:6], refs[6:14], refs[14:16], (), refs[16:])


def galerkin(part, sources, given, outputs, kept, scratch):
    own, other, k10, e10, onehot, index = sources
    if part == 0:
        ps, cs = outputs
        rs, l1s, l2s, r1s, r2s, e1s, e2s, ts, mids = scratch
    else:
        interp, coarse = outputs
        rs, l1s, l2s, r1s, r2s, e1s, e2s, ts, mids, ps, cs, sems = scratch
        early_ps, early_cs = given[0], given[1]

    def interp_copy(x, source):
        return pltpu.make_async_copy(
            source.at[pl.ds((x * 10 + 1) * 16, 128), :],
            interp.at[pl.ds((x - 1) * 128, 128), :],
            sems.at[x - 1],
        )

    def coarse_copy(x, source):
        return pltpu.make_async_copy(source.at[x - 1], coarse.at[x - 1], sems.at[7 + x])

    copies = []
    if part == 1:
        copies += [interp_copy(x, early_ps) for x in range(1, FULL)]
        copies += [coarse_copy(x, early_cs) for x in range(1, FULL - 1)]
        for copy in copies:
            copy.start()
    groups = range(GROUPS) if part == 0 else range(GROUPS, 13)
    batches = [groups[n : n + 4] for n in range(0, len(groups), 4)]
    first = lax.axis_index("vert") == 0
    lane16 = iota((16, 128), 1)
    sub16 = iota((16, 128), 0)
    lane8 = iota((8, 128), 1)
    sub8 = iota((8, 128), 0)
    block16, block8 = lane16 // 16, lane8 // 16
    lane128, sub128 = iota((128, 128), 1), iota((128, 128), 0)
    own_block = (lane128 % 64) // 8 == sub128 // 16
    ones = jnp.where(lane128 // 16 == sub128 // 16, 1.0, 0.0).astype(BF16)
    block_ones = [jnp.where(block16 == bb, 1.0, 0.0).astype(BF16) for bb in range(8)]
    on_diag = lane16 % 16 == sub16
    low128, high128 = z_weights(128)

    def rows_of(g):
        return slice(128 * g, 128 * g + 128)

    def fields(g):
        n = 8 if g < 12 else 4
        at = slice(8 * (g - groups[0]), 8 * (g - groups[0]) + n)
        a = own[at].reshape(n * 8, 128)
        b = other[at].reshape(n * 8, 128)
        fa, fb = jnp.where(first, a, b), jnp.where(first, b, a)
        if n == 8:
            return halves(jnp.concatenate([fa, fb], axis=0))
        none = jnp.zeros((32, 128), F32)
        return halves(jnp.concatenate([fa, none, fb, none], axis=0))

    def values(g, pair):
        oh = onehot[rows_of(g), :]
        return [jnp.where(own_block, product_t(oh, f), 0.0).astype(BF16) for f in pair]

    def rights(pair, spots):
        f1, f2 = pair
        c1, c2 = spots
        return product(
            jnp.concatenate([c1, c1, c2], axis=1), jnp.concatenate([f1, f2, f1], axis=0)
        )

    def system_of(g, right):
        spots = jnp.broadcast_to(index[g : g + 1, :], (16, 128))
        wanted = jnp.maximum(spots, 0)
        gram = jnp.zeros((16, 128), F32)
        for bb in range(8):
            part = gather_lanes(right[16 * bb : 16 * bb + 16, :], wanted)
            gram = jnp.where(block16 == bb, part, gram)
        gram = jnp.where(spots >= 0, gram, 0.0)
        d = jnp.where(on_diag, gram, 0.0)
        d = d[0:8, :] + d[8:16, :]
        for shift in (4, 2, 1):
            d = d + pltpu.roll(d, shift, 0)
        for bit in (1, 2, 4, 8):
            d = d + gather_lanes(d, lane8 ^ bit)
        ridge = (RIDGE / 16) * d + 1e-06
        ridge = jnp.concatenate([ridge, ridge], axis=0)
        system = gram + jnp.where(on_diag, ridge, 0.0)
        return [system[0:8, :], system[8:16, :]]

    systems = {}
    for batch in batches:
        pairs = [fields(g) for g in batch]
        spots = [values(g, pair) for g, pair in zip(batch, pairs)]
        found = [rights(pair, spot) for pair, spot in zip(pairs, spots)]
        for g, right in zip(batch, found):
            rs[rows_of(g), :] = right
        systems.update({g: system_of(g, right) for g, right in zip(batch, found)})

    for k in range(0, 16, 2):
        half, row = k // 8, k % 8
        at_0, at_1 = lane8 % 16 == k, lane8 % 16 == k + 1
        spot = block8 * 16 + k

        def row_of(t, row):
            return jnp.broadcast_to(t[row : row + 1, :], (8, 128))

        for s in systems.values():
            f0 = [gather_lanes(t, spot) for t in s]
            f1 = [gather_lanes(t, spot + 1) for t in s]
            a, b, c = row_of(f0[half], row), row_of(f1[half], row), row_of(f1[half], row + 1)
            inverse = 1.0 / (a * c - b * b)
            p0, p1 = row_of(s[half], row), row_of(s[half], row + 1)
            p0 = jnp.where(at_0, 1.0, jnp.where(at_1, 0.0, p0))
            p1 = jnp.where(at_1, 1.0, jnp.where(at_0, 0.0, p1))
            r0, r1 = (c * p0 - b * p1) * inverse, (a * p1 - b * p0) * inverse
            for t in range(2):
                new = jnp.where(at_0 | at_1, 0.0, s[t]) - f0[t] * r0 - f1[t] * r1
                if t == half:
                    new = jnp.where(sub8 == row, r0, jnp.where(sub8 == row + 1, r1, new))
                s[t] = new

    def weights(g):
        m1, m2 = halves(jnp.concatenate(systems[g], axis=0))
        m1 = jnp.concatenate([m1 * block_ones[bb] for bb in range(8)], axis=0)
        m2 = jnp.concatenate([m2 * block_ones[bb] for bb in range(8)], axis=0)
        r1, r2 = halves(rs[rows_of(g), :])
        w = product(
            jnp.concatenate([m1, m1, m2], axis=1), jnp.concatenate([r1, r2, r1], axis=0)
        )
        return w, product(ones, onehot[rows_of(g), :])

    def spread(ref, g):
        return jnp.concatenate(
            [jnp.broadcast_to(ref[8 * g + bb : 8 * g + bb + 1, :], (16, 128)) for bb in range(8)],
            axis=0,
        )

    def finish(g, w, c_row):
        p = w * (1.0 - c_row) + onehot[rows_of(g), :].astype(F32)
        ps[rows_of(g), :] = p
        left = spread(k10, g) * p
        padded = slice(128 * g + 160, 128 * g + 288)
        l1s[padded, :], l2s[padded, :] = halves(left)
        image = along_z(left, low128, high128)
        r1s[rows_of(g), :], r2s[rows_of(g), :] = halves(image)
        e1s[rows_of(g), :], e2s[rows_of(g), :] = halves(spread(e10, g) * p - image)

    for batch in batches:
        found = [weights(g) for g in batch]
        for g, pair in zip(batch, found):
            finish(g, *pair)

    moved = slice(KEPT.start + 160, KEPT.stop + 160)
    pieces = ((l1s, moved), (l2s, moved), (r1s, KEPT), (r2s, KEPT), (e1s, KEPT), (e2s, KEPT))
    if part == 0:
        for to, (ref, at) in zip(kept, pieces):
            to[...] = ref[at, :]
    else:
        for source, (ref, at) in zip(given[2:], pieces):
            ref[at, :] = source[...]
        ps[KEPT, :] = early_ps[KEPT, :]
        cs[FULL - 2, 0:6] = early_cs[FULL - 2, 0:6]
        late_copies = [interp_copy(x, ps) for x in range(FULL, 9)]
        for copy in late_copies:
            copy.start()
        copies += late_copies

    def wanted(x, source):
        return 1 <= x <= 8 and (max(x, source) < FULL) == (part == 0)

    def multiply(x, slot):
        base = x * 160
        used = [n for n in range(x - 1, x + 2) if wanted(n, x)]
        low, high = used[0], used[-1]

        def lefts(ref):
            return [ref[160 * n + 176 : 160 * n + 304, :] for n in range(low, high + 1)]

        def stacked(ref, order):
            return jnp.concatenate(
                [ref[base + 16 * y : base + 16 * y + 16, :] for y in order], axis=0
            )

        lhs = jnp.concatenate(
            [jnp.concatenate([a, a, b], axis=1) for a, b in zip(lefts(l1s), lefts(l2s))], axis=0
        )
        order = (0, 7, 6, 5, 4, 3, 2, 1, 8, 7, 6, 5, 4, 3, 2, 9)
        q1, q2 = stacked(r1s, order), stacked(r2s, order)
        at = 128 * (low - x + 1)
        ts[slot, at : at + 128 * (high - low + 1), :] = product_t(
            lhs, jnp.concatenate([q1, q2, q1], axis=1)
        )
        if wanted(x, x):
            order = (8, 7, 6, 5, 4, 3, 2, 1)
            q1, q2 = stacked(e1s, order), stacked(e2s, order)
            at = 128 * (x - low)
            mids[slot] = product_t(lhs[at : at + 128, :], jnp.concatenate([q1, q2, q1], axis=1))

    def arrange(x, slot):
        for side in range(3):
            ox = 1 - side
            if not wanted(x - ox, x):
                continue
            for o in range(3):
                first_turn, last_turn = min(o, 1), max(o - 1, 0)
                amount = (first_turn - o - block8) % 8
                scale = 1.0 if ox == 0 and o == 1 else (-1.0 if o == 1 else -WY)
                for half in range(2):
                    merged = jnp.zeros((8, 128), F32)
                    for y in range(8):
                        rows = slice(16 * y + 8 * half, 16 * y + 8 * half + 8)
                        if ox == 0 and o == 1:
                            part = mids[slot, rows, :]
                        else:
                            rows = slice(128 * side + rows.start, 128 * side + rows.stop)
                            if o == 2 or (o == 1 and y == 7):
                                part = ts[slot, rows, 128:256]
                            else:
                                part = ts[slot, rows, 0:128]
                        merged = jnp.where(block8 == (-y - o) % 8, part, merged)
                    merged = pltpu.roll(merged, 16 * first_turn, 1, stride=16, stride_axis=0)
                    for bit in (1, 2, 4):
                        merged = jnp.where(amount & bit != 0, pltpu.roll(merged, bit, 0), merged)
                    merged = pltpu.roll(merged, 16 * last_turn, 1, stride=16, stride_axis=0)
                    cs[x - ox - 1, 3 * (ox + 1) + o, :, half * 128 : half * 128 + 128] = scale * merged

    order = range(FULL) if part == 0 else range(FULL - 1, 10)
    multiply(order[0], 0)
    for n, x in enumerate(order):
        if n + 1 < len(order):
            multiply(x + 1, (n + 1) % 2)
        arrange(x, n % 2)
        if part == 1 and x >= FULL:
            copies.append(coarse_copy(x - 1, cs))
            copies[-1].start()
    for copy in copies:
        copy.wait()


def call(kernel, outs, scratch=(), specs=None, args=(), flops=0, outs_at=None, aliases=None):
    shapes = [jax.ShapeDtypeStruct(*o) for o in outs]
    moved = sum(a.size * 4 for a in args) + sum(4 * s.size for s in shapes)
    return pl.pallas_call(
        kernel,
        out_shape=shapes,
        in_specs=specs or [LOCAL] * len(args),
        out_specs=outs_at or [LOCAL] * len(outs),
        scratch_shapes=list(scratch),
        input_output_aliases=aliases or {},
        compiler_params=pltpu.CompilerParams(vmem_limit_bytes=48 << 20),
        cost_estimate=pl.CostEstimate(flops=flops, bytes_accessed=moved, transcendentals=0),
    )(*args)


def swapped(value, axis, first):
    count = lax.axis_size(axis)
    low = [(i, i + 1) for i in range(first, count - 1, 2)]
    return lax.ppermute(value, axis, low + [(j, i) for i, j in low])


def body(vectors, conductivity, c_points):
    tiles = jnp.transpose(vectors, (1, 2, 0, 3)).reshape(64, 8, 128)
    cond = conductivity
    padded, send1, send2, beside = call(
        pack_kernel,
        [((64, 128), F32), (SLAB, F32), (SLAB, F32), (SLAB, F32)],
        args=(tiles, cond, c_points.reshape(64, 16)),
    )
    got2 = swapped(send2, "gy", 1)
    got1 = swapped(send1, "gy", 0)
    far_own = swapped(beside, "gx", 1)
    (filled,) = call(middle_kernel, [(CROSS, F32)], args=(tiles, cond, padded))
    send1, send2 = call(
        cross_kernel, [(CROSS, F32), (SLAB, F32)], args=(filled, got1, got2), aliases={0: 0}
    )
    far_corner = swapped(send2, "gx", 1)
    near = swapped(send1, "gx", 0)
    rows = ((104, 128), F32)
    field_a, field_b, k10, e10, c10 = call(
        sweep_kernel,
        [((COLUMNS, 8, 128), F32), ((100 - COLUMNS, 8, 128), F32), rows, rows, rows],
        [VMEM((16, 16, 8, 128), F32)] * 2 + [VMEM((16, 16, 128), F32)] * 6,
        args=(tiles, cond, padded, got1, got2, near, far_own, far_corner),
    )
    pair = [(0, 1), (1, 0)]
    other_a = lax.ppermute(field_a, "vert", pair)
    other_b = lax.ppermute(field_b, "vert", pair)
    points = c10[:, 0:16].astype(jnp.int32)
    onehot = (points.reshape(1664, 1) == jnp.arange(128, dtype=jnp.int32)).astype(BF16)
    index = jnp.pad(points.reshape(13, 128), ((0, 3), (0, 0)))
    scratch = (
        [VMEM((1664, 128), F32)] + [VMEM((1920, 128), BF16)] * 2 + [VMEM((1664, 128), BF16)] * 4
        + [VMEM((2, 384, 256), F32), VMEM((2, 128, 128), F32)]
    )
    late_scratch = [
        VMEM((1664, 128), F32), VMEM((8, 9, 8, 256), F32), pltpu.SemaphoreType.DMA((16,)),
    ]
    kept = [((16 * COLUMNS, 128), F32), ((FULL - 1, 9, 8, 256), F32)] + [((SIZE, 128), BF16)] * 6
    kept = call(
        early_kernel, kept, scratch, args=(field_a, other_a, k10, e10, onehot, index)
    )
    interp, coarse = call(
        late_kernel,
        [((1024, 128), F32), ((8, 9, 8, 256), F32)],
        scratch + late_scratch,
        outs_at=[FAR] * 2,
        args=(field_b, other_b, k10, e10, onehot, index, *kept),
    )
    return interp.reshape(8, 8, 16, 128), jnp.transpose(coarse, (0, 2, 1, 3))


def solution(mesh):
    placed = (P("vert", "gx", "gy", None), P("gx", "gy", None), P("gx", "gy", None))
    return jax.shard_map(
        body,
        mesh=mesh,
        in_specs=placed,
        out_specs=(P("gx", "gy", None, None), P("gx", "gy", None, None)),
        check_vma=False,
    )
```
